32 devices in a mesh: ctx: 16 (over z, x, core), fsdp: 2 (over y).
Axes of the slice: x: 2, y: 2, z: 4, core: 2. Of those that a mesh axis runs over, the one named last changes fastest.
Arguments:
- query_heads: bfloat16 [1024, 3072], P(('ctx', 'fsdp')), may hold values from -6 to 6
- kv_latent: bfloat16 [1024, 576], P(('ctx', 'fsdp')), may hold values from -800 to 800
- w_uk: bfloat16 [512, 2048], P('ctx', 'fsdp'), may hold values from -0.25 to 0.25
- w_uv: bfloat16 [512, 2048], P('ctx', 'fsdp'), may hold values from -0.25 to 0.25
- span_order: int32 [32], replicated, may hold values from 0 to 31, each once
Outputs:
- attn_out: bfloat16 [1024, 2048], P(('ctx', 'fsdp'))
The draws below stay inside these ranges and needn't reach their ends.
Inputs may be any that keep to these rules, and one draw needn't show every extreme that they name: `span_order`: each span number appears exactly once.
All inputs are finite; a program needn't handle non-finite values.
Results may differ from the reference program's by a relative error of at most 0.01.
The reference program's roundings to bfloat16 on the way count: a program that leaves them out, or rounds other values in their place, can miss the bound.
Values may be sent and summed in bfloat16 or wider, within the bound.
A program may use at most 64 MiB of HBM per device.

```python
import math
import jax
import jax.numpy as jnp
from jax import lax

LATENT = 512
ROPE = 64
NOPE = 128
VDIM = 128
SPAN = 32
HEADS = 16
TOKENS = 1024
N_CTX = 16


def draw_kv_latent(key, part):
    row_total = TOKENS
    col_total = LATENT + ROPE
    key_base = jax.random.fold_in(jax.random.fold_in(key, 17), 0)
    base_vals = jax.random.truncated_normal(key_base, -4.0, 4.0, (row_total, col_total), jnp.float32)
    return base_vals.astype(jnp.bfloat16)


def level_of(key, dims, cuts, least, top_value):
    loudness = 1.0
    for axis_at, blocks in cuts:
        steps = jax.random.uniform(jax.random.fold_in(jax.random.fold_in(key, 6), axis_at), (blocks,), jnp.float32, least / len(cuts), top_value / len(cuts))
        loudness = loudness * jnp.repeat(jnp.exp(steps), dims[axis_at] // blocks).reshape((-1,) + (1,) * (len(dims) - 1 - axis_at))
    return loudness


def centred(rng, extent, spread, most, pieces=(), kind=jnp.bfloat16):
    array = spread * jax.random.normal(rng, extent, jnp.float32)
    if pieces:
        array = array * level_of(rng, extent, pieces, -0.22, 0.18)
    return jnp.clip(array, -most, most).astype(kind)


def setup_inputs(seed: int = 0) -> dict:
    arg_keys = jax.random.split(jax.random.key(seed), 6)
    query_heads = centred(arg_keys[0], (TOKENS, HEADS * (NOPE + ROPE)), 1.0, 6.0, ((0, 32),))
    kv_latent = draw_kv_latent(jax.random.fold_in(arg_keys[5], 71), 0)
    w_uk = centred(arg_keys[2], (LATENT, HEADS * NOPE), LATENT ** -0.5, 0.25, ((0, 16), (1, 2)))
    w_uv = centred(arg_keys[3], (LATENT, HEADS * VDIM), LATENT ** -0.5, 0.25, ((0, 16), (1, 2)))
    span_order = jax.random.permutation(arg_keys[4], 2 * N_CTX).astype(jnp.int32)
    return dict(query_heads=query_heads, kv_latent=kv_latent, w_uk=w_uk, w_uv=w_uv, span_order=span_order)


def positions(span_order, row_total):
    row_ids = jnp.arange(row_total, dtype=jnp.int32)
    return (span_order[row_ids // SPAN] * SPAN + row_ids % SPAN).astype(jnp.int32)

def rotary_tables(position_ids):
    half_width = ROPE // 2
    frequency = 10000.0 ** (-jnp.arange(half_width, dtype=jnp.float32) / half_width)
    angles = position_ids.astype(jnp.float32)[:, None] * frequency[None, :]
    return (jnp.cos(angles), jnp.sin(angles))

def rotate(values, cos_table, sin_table):
    half_width = ROPE // 2
    values = values.astype(jnp.float32)
    first_half = values[..., :half_width]
    second_half = values[..., half_width:]
    turned = jnp.concatenate([first_half * cos_table - second_half * sin_table, second_half * cos_table + first_half * sin_table], axis=-1)
    return turned.astype(jnp.bfloat16)

def reference(query_heads, kv_latent, w_uk, w_uv, span_order):
    pos = positions(span_order, TOKENS)
    cos_table, sin_table = rotary_tables(pos)
    latent = kv_latent[:, :LATENT]
    keys = jnp.concatenate([latent, rotate(kv_latent[:, LATENT:], cos_table, sin_table)], axis=1)
    allowed = pos[None, :] <= pos[:, None]
    score_scale = 1.0 / math.sqrt(NOPE + ROPE)
    queries = query_heads.reshape(TOKENS, HEADS, NOPE + ROPE).transpose(1, 0, 2)
    key_maps = w_uk.reshape(LATENT, HEADS, NOPE).transpose(1, 0, 2)
    value_maps = w_uv.reshape(LATENT, HEADS, VDIM).transpose(1, 0, 2)

    def one_head(params):
        head_query, head_keymap, head_valmap = params
        query_latent = jnp.dot(head_query[:, :NOPE], head_keymap.T, preferred_element_type=jnp.float32).astype(jnp.bfloat16)
        query_rope = rotate(head_query[:, NOPE:], cos_table, sin_table)
        query_full = jnp.concatenate([query_latent, query_rope], axis=1)
        score = jnp.dot(query_full, keys.T, preferred_element_type=jnp.float32) * score_scale
        score = jnp.where(allowed, score, jnp.float32(-1e+30))
        row_max = lax.optimization_barrier(jnp.max(score, axis=1, keepdims=True))
        exp_vals = jnp.where(allowed, jnp.exp(score - row_max), jnp.float32(0.0))
        weights = exp_vals.astype(jnp.bfloat16)
        totals = lax.optimization_barrier(jnp.sum(exp_vals, axis=1, keepdims=True))
        out_latent = (jnp.dot(weights, latent, preferred_element_type=jnp.float32) / totals).astype(jnp.bfloat16)
        return jnp.dot(out_latent, head_valmap, preferred_element_type=jnp.float32).astype(jnp.bfloat16)
    head_outs = lax.map(one_head, (queries, key_maps, value_maps))
    return head_outs.transpose(1, 0, 2).reshape(TOKENS, HEADS * VDIM)
```

```python
import functools
import math

import jax
import jax.numpy as jnp
import numpy as np
from jax import lax
from jax.experimental import pallas as pl
from jax.experimental.pallas import tpu as pltpu
from jax.sharding import PartitionSpec as P

LATENT = 512
ROPE = 64
NOPE = 128
VDIM = 128
SPAN = 32


def lookup(entries, wanted):
    matches = wanted[:, None] == jnp.arange(entries.shape[0], dtype=jnp.int32)[None, :]
    return jnp.sum(jnp.where(matches, entries[None, :], 0), axis=1)


def position(span_order, row_ids):
    return lookup(span_order, row_ids // SPAN) * SPAN + row_ids % SPAN


def rotary_tables(position_ids):
    half_width = ROPE // 2
    frequency = 10000.0 ** (-jnp.arange(half_width, dtype=jnp.float32) / half_width)
    angles = position_ids.astype(jnp.float32)[:, None] * frequency[None, :]
    return (jnp.cos(angles), jnp.sin(angles))


def rotate(values, cos_table, sin_table):
    half_width = ROPE // 2
    values = values.astype(jnp.float32)
    first_half = values[..., :half_width]
    second_half = values[..., half_width:]
    turned = jnp.concatenate(
        [
            first_half * cos_table - second_half * sin_table,
            second_half * cos_table + first_half * sin_table,
        ],
        axis=-1,
    )
    return turned.astype(jnp.bfloat16)


def body(query_heads, kv_latent, w_uk, w_uv, span_order):
    ctx_index = lax.axis_index("ctx")
    fsdp_index = lax.axis_index("fsdp")
    fsdp_count = lax.axis_size("fsdp")
    local_count = kv_latent.shape[0]
    row_count = local_count * fsdp_count
    score_scale = 1.0 / math.sqrt(NOPE + ROPE)
    queries = lax.all_to_all(query_heads, "fsdp", split_axis=1, concat_axis=0, tiled=True)
    head_count = queries.shape[1] // (NOPE + ROPE)
    queries = queries.reshape(row_count, head_count, NOPE + ROPE)
    key_map, value_map = (
        lax.all_gather(w_uk, "ctx", axis=0, tiled=True),
        lax.all_gather(w_uv, "ctx", axis=0, tiled=True),
    )
    query_pos = position(span_order, ctx_index * row_count + jnp.arange(row_count, dtype=jnp.int32))
    own_ids = (
        ctx_index * row_count + fsdp_index * local_count + jnp.arange(local_count, dtype=jnp.int32)
    )
    own_cos, own_sin = rotary_tables(position(span_order, own_ids))
    local_keys = jnp.concatenate(
        [kv_latent[:, :LATENT], rotate(kv_latent[:, LATENT:], own_cos, own_sin)], axis=1
    )
    query_cos, query_sin = rotary_tables(query_pos)
    query_latent = jnp.einsum(
        "rhd,nhd->rhn",
        queries[:, :, :NOPE],
        key_map.reshape(LATENT, head_count, NOPE),
        preferred_element_type=jnp.float32,
    ).astype(jnp.bfloat16)
    query_rope = rotate(queries[:, :, NOPE:], query_cos[:, None, :], query_sin[:, None, :])
    query_full = jnp.concatenate([query_latent, query_rope], axis=2)
    segment = lax.all_gather(local_keys, ("ctx", "fsdp"), axis=0, tiled=True)
    key_pos = position(span_order, jnp.arange(segment.shape[0], dtype=jnp.int32))
    row_max = jnp.full((row_count, head_count), -1e30, jnp.float32)
    totals = jnp.zeros((row_count, head_count), jnp.float32)
    accum = jnp.zeros((row_count, head_count, LATENT), jnp.float32)
    seg_count = segment.shape[0]
    for sub_begin in range(0, seg_count, 1024):
        sub_keys = segment[sub_begin : sub_begin + 1024]
        sub_pos = key_pos[sub_begin : sub_begin + 1024]
        allowed = (sub_pos[None, :] <= query_pos[:, None])[:, None, :]
        score_block = (
            jnp.einsum("rhe,ke->rhk", query_full, sub_keys, preferred_element_type=jnp.float32)
            * score_scale
        )
        score_block = jnp.where(allowed, score_block, jnp.float32(-1e30))
        new_max = jnp.maximum(row_max, jnp.max(score_block, axis=2))
        exp_vals = jnp.where(allowed, jnp.exp(score_block - new_max[:, :, None]), jnp.float32(0.0))
        rescale = jnp.exp(row_max - new_max)
        totals = totals * rescale + jnp.sum(exp_vals, axis=2)
        accum = accum * rescale[:, :, None] + jnp.einsum(
            "rhk,kn->rhn",
            exp_vals.astype(jnp.bfloat16),
            sub_keys[:, :LATENT],
            preferred_element_type=jnp.float32,
        )
        row_max = new_max
    row_max, totals, accum = (row_max, totals, accum)
    out_latent = (accum / totals[:, :, None]).astype(jnp.bfloat16)
    head_out = jnp.einsum(
        "rhn,nhd->rhd",
        out_latent,
        value_map.reshape(LATENT, head_count, VDIM),
        preferred_element_type=jnp.float32,
    ).astype(jnp.bfloat16)
    head_out = head_out.reshape(row_count, head_count * VDIM)
    return lax.all_to_all(head_out, "fsdp", split_axis=0, concat_axis=1, tiled=True)


MESH = pl.DeviceIdType.MESH


def rope_table(count):
    half_width = ROPE // 2
    frequency = np.float32(10000.0) ** (-np.arange(half_width, dtype=np.float32) / half_width)
    angles = np.arange(count, dtype=np.float32)[:, None] * frequency[None, :].astype(np.float32)
    cos, sin = np.cos(angles), np.sin(angles)
    return np.concatenate([cos, cos, -sin, sin], axis=1).astype(np.float32)


def turn(values, table):
    half_width = ROPE // 2
    values = values.astype(jnp.float32)
    swapped = jnp.concatenate([values[:, half_width:], values[:, :half_width]], axis=1)
    return (values * table[:, :ROPE] + swapped * table[:, ROPE:]).astype(jnp.bfloat16)


def kernel(
    span, q, kv, wuk, wuv, tab, out,
    qb, kb, wkb, wvb, ob,
    loc, ks, kr, sks, skr, wxs, wxr, wzs, wr, wss, wsr, qs, qr, os_, or_,
):
    depth = kb.shape[0]
    heads = 4
    width = heads * NOPE
    q_width = heads * (NOPE + ROPE)
    ctx = lax.axis_index("ctx")
    f = lax.axis_index("fsdp")
    c = lax.rem(ctx, 2)
    x = lax.rem(lax.div(ctx, 2), 2)
    z = lax.div(ctx, 4)

    def dev(z_, x_, c_, f_):
        return ((z_ * 2 + x_) * 2 + c_, f_)

    plane = [(1 - x, f), (x, 1 - f), (1 - x, 1 - f)]
    cols = [(x, f)] + plane
    peers = [dev(z, px, c, pf) for px, pf in plane]
    sib = dev(z, x, 1 - c, f)
    up = dev(z + 1, x, c, f)
    down = dev(z - 1, x, c, f)
    has_up = z < depth - 1
    has_down = z > 0

    def rc(src, dst, ssem, rsem, device):
        return pltpu.make_async_remote_copy(
            src_ref=src, dst_ref=dst, send_sem=ssem, recv_sem=rsem,
            device_id=device, device_id_type=MESH,
        )

    def lanes(index, size):
        return pl.ds(pl.multiple_of(index * size, 128), size)

    group = f * 2 + x
    me = x * 2 + f
    own = [
        pltpu.make_async_copy(wuk.at[:, lanes(x, width)], wkb.at[z, x, c], loc.at[0]),
        pltpu.make_async_copy(wuv.at[:, lanes(x, width)], wvb.at[z, x, c], loc.at[1]),
        pltpu.make_async_copy(q.at[:, lanes(group, q_width)], qb.at[me], loc.at[2]),
    ]

    barrier = pltpu.get_barrier_semaphore()
    for device in peers + [sib]:
        pl.semaphore_signal(barrier, inc=1, device_id=device, device_id_type=MESH)

    @pl.when(has_up)
    def _():
        pl.semaphore_signal(barrier, inc=1, device_id=up, device_id_type=MESH)

    @pl.when(has_down)
    def _():
        pl.semaphore_signal(barrier, inc=1, device_id=down, device_id_type=MESH)

    for copy in own:
        copy.start()
    own_tab = tab[span[ctx * 2 + f]]
    kb[z, x, c, f, :, :LATENT] = kv[:, :LATENT]
    kb[z, x, c, f, :, LATENT:] = turn(kv[:, LATENT:], own_tab)

    pl.semaphore_wait(barrier, 4 + lax.min(z, 1) + lax.min(depth - 1 - z, 1))

    def k_up(zi):
        block = kb.at[zi, x, c, f]
        return rc(block, block, ks.at[zi, 0], kr.at[zi, 0], up)

    def k_down(zi):
        block = kb.at[zi, x, c, f]
        return rc(block, block, ks.at[zi, 1], kr.at[zi, 0], down)

    def k_plane(zi, kind):
        block = kb.at[zi, x, c, f]
        return rc(block, block, ks.at[zi, 2 + kind], kr.at[zi, 1 + kind], peers[kind])

    def k_plane_in(zi, kind):
        block = kb.at[zi, plane[kind][0], c, plane[kind][1]]
        return rc(block, block, ks.at[zi, 2 + kind], kr.at[zi, 1 + kind], peers[kind])

    def k_sib(col, core):
        block = kb.at[:, cols[col][0], core, cols[col][1]]
        return rc(block, block, sks.at[col], skr.at[col], sib)

    sources = (wuk, wuv)
    bufs = (wkb, wvb)

    def w_x(m):
        return rc(
            sources[m].at[:, lanes(1 - x, width)], bufs[m].at[z, x, c], wxs.at[m], wxr.at[m], peers[0]
        )

    def w_up(m, zi):
        block = bufs[m].at[zi, :, c]
        return rc(block, block, wzs.at[m, zi, 0], wr.at[m, zi], up)

    def w_down(m, zi):
        block = bufs[m].at[zi, :, c]
        return rc(block, block, wzs.at[m, zi, 1], wr.at[m, zi], down)

    def w_sib(m, zi, core):
        block = bufs[m].at[zi, :, core]
        return rc(block, block, wss.at[m, zi], wsr.at[m, zi], sib)

    def q_send(kind):
        px, pf = plane[kind]
        return rc(
            q.at[:, lanes(pf * 2 + px, q_width)], qb.at[me], qs.at[kind], qr.at[kind], peers[kind]
        )

    def q_in(kind):
        px, pf = plane[kind]
        block = qb.at[px * 2 + pf]
        return rc(block, block, qs.at[kind], qr.at[kind], peers[kind])

    def each_round(step, on_low, on_high):
        pl.when(z - step >= 0)(lambda: on_low(z - step))
        pl.when(z + step < depth)(lambda: on_high(z + step))

    def k_low(zi):
        k_up(zi).wait_recv()
        pl.when(has_up)(lambda: k_up(zi).start())
        for kind in range(3):
            k_plane(zi, kind).start()

    def k_high(zi):
        k_down(zi).wait_recv()
        pl.when(has_down)(lambda: k_down(zi).start())
        for kind in range(3):
            k_plane(zi, kind).start()

    def w_low(m, zi):
        w_up(m, zi).wait_recv()
        pl.when(has_up)(lambda: w_up(m, zi).start())
        w_sib(m, zi, c).start()

    def w_high(m, zi):
        w_down(m, zi).wait_recv()
        pl.when(has_down)(lambda: w_down(m, zi).start())
        w_sib(m, zi, c).start()

    def k_round(step):
        each_round(step, k_low, k_high)

    def w_round(m, step):
        each_round(step, functools.partial(w_low, m), functools.partial(w_high, m))

    def w_first(m):
        rc(bufs[m].at[z, 1 - x, c], bufs[m].at[z, 1 - x, c], wxs.at[m], wxr.at[m], peers[0]).wait_recv()
        pl.when(has_up)(lambda: w_up(m, z).start())
        pl.when(has_down)(lambda: w_down(m, z).start())
        w_sib(m, z, c).start()

    w_x(0).start()
    pl.when(has_up)(lambda: k_up(z).start())
    pl.when(has_down)(lambda: k_down(z).start())
    for kind in range(3):
        k_plane(z, kind).start()
    w_x(1).start()
    for kind in range(3):
        q_send(kind).start()
    for copy in own:
        copy.wait()
    w_first(0)
    k_round(1)
    w_round(0, 1)
    w_first(1)
    for step in range(2, depth):
        k_round(step)
        w_round(0, step)
    k_sib(0, c).start()
    for kind in range(3):
        for zi in range(depth):
            k_plane_in(zi, kind).wait_recv()
        k_sib(1 + kind, c).start()
    w_round(1, 1)
    for kind in range(3):
        q_in(kind).wait_recv()
    for zi in range(depth):
        w_sib(0, zi, 1 - c).wait_recv()

    rows = 4 * SPAN
    tables = []
    places = []
    for px in range(2):
        for pf in range(2):
            held = span[((z * 2 + px) * 2 + c) * 2 + pf]
            tables.append(tab[held])
            places.append(held * SPAN + lax.broadcasted_iota(jnp.int32, (SPAN, 1), 0))
    table = jnp.concatenate(tables, axis=0)
    query_pos = jnp.concatenate(places, axis=0)
    queries = qb[...].reshape(rows, q_width)
    key_map = wkb[...].reshape(LATENT, width)
    lat, rot = [], []
    for head in range(heads):
        begin = head * (NOPE + ROPE)
        lat.append(
            lax.dot_general(
                queries[:, begin : begin + NOPE],
                key_map[:, head * NOPE : (head + 1) * NOPE],
                (((1,), (1,)), ((), ())),
                preferred_element_type=jnp.float32,
            ).astype(jnp.bfloat16)
        )
        rot.append(turn(queries[:, begin + NOPE : begin + NOPE + ROPE], table))
    total_keys = depth * 8 * SPAN
    lane = lax.broadcasted_iota(jnp.int32, (1, total_keys), 1)
    key_pos = jnp.zeros((1, total_keys), jnp.int32)
    for slot in range(depth * 8):
        key_pos = jnp.where(lane // SPAN == slot, span[slot] * SPAN, key_pos)
    key_pos = key_pos + lane % SPAN
    allowed = key_pos <= query_pos

    for step in range(2, depth):
        w_round(1, step)
    for col in range(4):
        k_sib(col, 1 - c).wait_recv()

    keys_lat = kb[:, :, :, :, :, :LATENT].reshape(total_keys, LATENT)
    keys_rot = kb[:, :, :, :, :, LATENT:].reshape(total_keys, ROPE)
    scale = 1.0 / math.sqrt(NOPE + ROPE)
    outs = []
    for pair in range(2):
        pick = slice(2 * pair, 2 * pair + 2)
        score = lax.dot_general(
            jnp.concatenate(lat[pick], axis=0), keys_lat,
            (((1,), (1,)), ((), ())), preferred_element_type=jnp.float32,
        ) + lax.dot_general(
            jnp.concatenate(rot[pick], axis=0), keys_rot,
            (((1,), (1,)), ((), ())), preferred_element_type=jnp.float32,
        )
        score = jnp.where(
            allowed[None], score.reshape(2, rows, total_keys) * scale, jnp.float32(-1e30)
        ).reshape(2 * rows, total_keys)
        expo = jnp.exp(score - jnp.max(score, axis=1, keepdims=True))
        totals = jnp.sum(expo, axis=1, keepdims=True)
        accum = jnp.dot(expo.astype(jnp.bfloat16), keys_lat, preferred_element_type=jnp.float32)
        outs.append((accum * (1.0 / totals)).astype(jnp.bfloat16))

    for zi in range(depth):
        w_sib(1, zi, 1 - c).wait_recv()

    value_map = wvb[...].reshape(LATENT, width)
    for head in range(heads):
        part = outs[head // 2][(head % 2) * rows : (head % 2 + 1) * rows]
        ob[:, :, head * VDIM : (head + 1) * VDIM] = (
            jnp.dot(
                part, value_map[:, head * VDIM : (head + 1) * VDIM],
                preferred_element_type=jnp.float32,
            )
            .astype(jnp.bfloat16)
            .reshape(4, SPAN, VDIM)
        )

    def o_send(kind):
        px, pf = plane[kind]
        return rc(
            ob.at[px * 2 + pf], out.at[:, lanes(group, width)], os_.at[kind], or_.at[kind], peers[kind]
        )

    def o_in(kind):
        px, pf = plane[kind]
        block = out.at[:, lanes(pf * 2 + px, width)]
        return rc(block, block, os_.at[kind], or_.at[kind], peers[kind])

    for kind in range(3):
        o_send(kind).start()
    mine = pltpu.make_async_copy(ob.at[me], out.at[:, lanes(group, width)], loc.at[0])
    mine.start()

    for zi in range(depth):
        pl.when(jnp.logical_and(has_up, zi <= z))(lambda zi=zi: k_up(zi).wait_send())
        pl.when(jnp.logical_and(has_down, zi >= z))(lambda zi=zi: k_down(zi).wait_send())
        for kind in range(3):
            k_plane(zi, kind).wait_send()
        for m in range(2):
            pl.when(jnp.logical_and(has_up, zi <= z))(lambda zi=zi, m=m: w_up(m, zi).wait_send())
            pl.when(jnp.logical_and(has_down, zi >= z))(lambda zi=zi, m=m: w_down(m, zi).wait_send())
            w_sib(m, zi, c).wait_send()
    for m in range(2):
        w_x(m).wait_send()
    for col in range(4):
        k_sib(col, c).wait_send()
    for kind in range(3):
        q_send(kind).wait_send()
    mine.wait()
    for kind in range(3):
        o_in(kind).wait_recv()
        o_send(kind).wait_send()


def planned(query_heads, kv_latent, w_uk, w_uv, span_order):
    depth = lax.axis_size("ctx") // 4
    local_count = kv_latent.shape[0]
    width = w_uk.shape[1] // 2
    q_width = query_heads.shape[1] // 4
    dma = pltpu.SemaphoreType.DMA
    vmem = pl.BlockSpec(memory_space=pltpu.VMEM)
    spans = span_order.shape[0]
    table = jnp.asarray(rope_table(spans * SPAN).reshape(spans, SPAN, 2 * ROPE))
    return pl.pallas_call(
        kernel,
        out_shape=jax.ShapeDtypeStruct((local_count, width * 4), jnp.bfloat16),
        in_specs=[pl.BlockSpec(memory_space=pltpu.SMEM)] + [vmem] * 5,
        out_specs=vmem,
        scratch_shapes=[
            pltpu.VMEM((4, SPAN, q_width), jnp.bfloat16),
            pltpu.VMEM((depth, 2, 2, 2, SPAN, LATENT + ROPE), jnp.bfloat16),
            pltpu.VMEM((depth, 2, 2, w_uk.shape[0], width), jnp.bfloat16),
            pltpu.VMEM((depth, 2, 2, w_uk.shape[0], width), jnp.bfloat16),
            pltpu.VMEM((4, SPAN, width), jnp.bfloat16),
            dma((3,)),
            dma((depth, 5)), dma((depth, 4)), dma((4,)), dma((4,)),
            dma((2,)), dma((2,)), dma((2, depth, 2)), dma((2, depth)), dma((2, depth)), dma((2, depth)),
            dma((3,)), dma((3,)), dma((3,)), dma((3,)),
        ],
        compiler_params=pltpu.CompilerParams(
            collective_id=0, has_side_effects=True, vmem_limit_bytes=48 * 1024 * 1024
        ),
        name="mla_prefill",
    )(span_order, query_heads, kv_latent, w_uk, w_uv, table)


def solution(mesh):
    placed = (
        P(("ctx", "fsdp"), None),
        P(("ctx", "fsdp"), None),
        P("ctx", "fsdp"),
        P("ctx", "fsdp"),
        P(),
    )
    small = mesh.shape["fsdp"] == 2 and mesh.shape["ctx"] == 16

    def program(query_heads, kv_latent, w_uk, w_uv, span_order):
        fits = (
            small
            and query_heads.shape[1] == 16 * (NOPE + ROPE)
            and query_heads.shape[0] == 32 * SPAN
        )
        return jax.shard_map(
            planned if fits else body,
            mesh=mesh, in_specs=placed, out_specs=P(("ctx", "fsdp"), None), check_vma=False,
        )(query_heads, kv_latent, w_uk, w_uv, span_order)

    return program
```

```python
import functools
import math

import jax
import jax.numpy as jnp
import numpy as np
from jax import lax
from jax.experimental import pallas as pl
from jax.experimental.pallas import tpu as pltpu
from jax.sharding import PartitionSpec as P

LATENT = 512
ROPE = 64
NOPE = 128
VDIM = 128
SPAN = 32


def lookup(entries, wanted):
    matches = wanted[:, None] == jnp.arange(entries.shape[0], dtype=jnp.int32)[None, :]
    return jnp.sum(jnp.where(matches, entries[None, :], 0), axis=1)


def position(span_order, row_ids):
    return lookup(span_order, row_ids // SPAN) * SPAN + row_ids % SPAN


def rotary_tables(position_ids):
    half_width = ROPE // 2
    frequency = 10000.0 ** (-jnp.arange(half_width, dtype=jnp.float32) / half_width)
    angles = position_ids.astype(jnp.float32)[:, None] * frequency[None, :]
    return (jnp.cos(angles), jnp.sin(angles))


def rotate(values, cos_table, sin_table):
    half_width = ROPE // 2
    values = values.astype(jnp.float32)
    first_half = values[..., :half_width]
    second_half = values[..., half_width:]
    turned = jnp.concatenate(
        [
            first_half * cos_table - second_half * sin_table,
            second_half * cos_table + first_half * sin_table,
        ],
        axis=-1,
    )
    return turned.astype(jnp.bfloat16)


def body(query_heads, kv_latent, w_uk, w_uv, span_order):
    ctx_index = lax.axis_index("ctx")
    fsdp_index = lax.axis_index("fsdp")
    fsdp_count = lax.axis_size("fsdp")
    local_count = kv_latent.shape[0]
    row_count = local_count * fsdp_count
    score_scale = 1.0 / math.sqrt(NOPE + ROPE)
    queries = lax.all_to_all(query_heads, "fsdp", split_axis=1, concat_axis=0, tiled=True)
    head_count = queries.shape[1] // (NOPE + ROPE)
    queries = queries.reshape(row_count, head_count, NOPE + ROPE)
    key_map, value_map = (
        lax.all_gather(w_uk, "ctx", axis=0, tiled=True),
        lax.all_gather(w_uv, "ctx", axis=0, tiled=True),
    )
    query_pos = position(span_order, ctx_index * row_count + jnp.arange(row_count, dtype=jnp.int32))
    own_ids = (
        ctx_index * row_count + fsdp_index * local_count + jnp.arange(local_count, dtype=jnp.int32)
    )
    own_cos, own_sin = rotary_tables(position(span_order, own_ids))
    local_keys = jnp.concatenate(
        [kv_latent[:, :LATENT], rotate(kv_latent[:, LATENT:], own_cos, own_sin)], axis=1
    )
    query_cos, query_sin = rotary_tables(query_pos)
    query_latent = jnp.einsum(
        "rhd,nhd->rhn",
        queries[:, :, :NOPE],
        key_map.reshape(LATENT, head_count, NOPE),
        preferred_element_type=jnp.float32,
    ).astype(jnp.bfloat16)
    query_rope = rotate(queries[:, :, NOPE:], query_cos[:, None, :], query_sin[:, None, :])
    query_full = jnp.concatenate([query_latent, query_rope], axis=2)
    segment = lax.all_gather(local_keys, ("ctx", "fsdp"), axis=0, tiled=True)
    key_pos = position(span_order, jnp.arange(segment.shape[0], dtype=jnp.int32))
    row_max = jnp.full((row_count, head_count), -1e30, jnp.float32)
    totals = jnp.zeros((row_count, head_count), jnp.float32)
    accum = jnp.zeros((row_count, head_count, LATENT), jnp.float32)
    seg_count = segment.shape[0]
    for sub_begin in range(0, seg_count, 1024):
        sub_keys = segment[sub_begin : sub_begin + 1024]
        sub_pos = key_pos[sub_begin : sub_begin + 1024]
        allowed = (sub_pos[None, :] <= query_pos[:, None])[:, None, :]
        score_block = (
            jnp.einsum("rhe,ke->rhk", query_full, sub_keys, preferred_element_type=jnp.float32)
            * score_scale
        )
        score_block = jnp.where(allowed, score_block, jnp.float32(-1e30))
        new_max = jnp.maximum(row_max, jnp.max(score_block, axis=2))
        exp_vals = jnp.where(allowed, jnp.exp(score_block - new_max[:, :, None]), jnp.float32(0.0))
        rescale = jnp.exp(row_max - new_max)
        totals = totals * rescale + jnp.sum(exp_vals, axis=2)
        accum = accum * rescale[:, :, None] + jnp.einsum(
            "rhk,kn->rhn",
            exp_vals.astype(jnp.bfloat16),
            sub_keys[:, :LATENT],
            preferred_element_type=jnp.float32,
        )
        row_max = new_max
    row_max, totals, accum = (row_max, totals, accum)
    out_latent = (accum / totals[:, :, None]).astype(jnp.bfloat16)
    head_out = jnp.einsum(
        "rhn,nhd->rhd",
        out_latent,
        value_map.reshape(LATENT, head_count, VDIM),
        preferred_element_type=jnp.float32,
    ).astype(jnp.bfloat16)
    head_out = head_out.reshape(row_count, head_count * VDIM)
    return lax.all_to_all(head_out, "fsdp", split_axis=0, concat_axis=1, tiled=True)


MESH = pl.DeviceIdType.MESH


def rope_table(count, stride):
    half_width = ROPE // 2
    frequency = 10000.0 ** (-np.arange(half_width, dtype=np.float64) / half_width)
    angles = np.arange(count)[:, None] * stride * frequency[None, :]
    cos, sin = np.cos(angles), np.sin(angles)
    return np.concatenate([cos, cos, sin, sin], axis=1).astype(np.float32)


def span_table(coarse, fine):
    cos = coarse[:, :ROPE] * fine[:, :ROPE] - coarse[:, ROPE:] * fine[:, ROPE:]
    sin = coarse[:, ROPE:] * fine[:, :ROPE] + coarse[:, :ROPE] * fine[:, ROPE:]
    first = lax.broadcasted_iota(jnp.int32, sin.shape, 1) < ROPE // 2
    return cos, jnp.where(first, -sin, sin)


def turn(values, cos, sin):
    half_width = ROPE // 2
    values = values.astype(jnp.float32)
    swapped = jnp.concatenate([values[:, half_width:], values[:, :half_width]], axis=1)
    return (values * cos + swapped * sin).astype(jnp.bfloat16)


def kernel(
    span_hbm, q, kv, wuk, wuv, coarse_hbm, fine_hbm, out,
    span, coarse, fine, qb, kb, wkb, wvb, ob,
    loc, ks, kr, sks, skr, wxs, wxr, wzs, wr, wss, wsr, qs, qr, os_, or_,
):
    depth = kb.shape[0]
    heads = 4
    width = heads * NOPE
    q_width = heads * (NOPE + ROPE)
    ctx = lax.axis_index("ctx")
    f = lax.axis_index("fsdp")
    c = lax.rem(ctx, 2)
    x = lax.rem(lax.div(ctx, 2), 2)
    z = lax.div(ctx, 4)

    def dev(z_, x_, c_, f_):
        return ((z_ * 2 + x_) * 2 + c_, f_)

    plane = [(1 - x, f), (x, 1 - f), (1 - x, 1 - f)]
    cols = [(x, f)] + plane
    peers = [dev(z, px, c, pf) for px, pf in plane]
    sib = dev(z, x, 1 - c, f)
    up = dev(z + 1, x, c, f)
    down = dev(z - 1, x, c, f)
    has_up = z < depth - 1
    has_down = z > 0

    def rc(src, dst, ssem, rsem, device):
        return pltpu.make_async_remote_copy(
            src_ref=src, dst_ref=dst, send_sem=ssem, recv_sem=rsem,
            device_id=device, device_id_type=MESH,
        )

    def lanes(index, size):
        return pl.ds(pl.multiple_of(index * size, 128), size)

    group = f * 2 + x
    me = x * 2 + f
    early = [
        pltpu.make_async_copy(kv, kb.at[z, x, c, f], loc.at[3]),
        pltpu.make_async_copy(span_hbm, span, loc.at[4]),
        pltpu.make_async_copy(coarse_hbm, coarse, loc.at[5]),
        pltpu.make_async_copy(fine_hbm, fine, loc.at[6]),
    ]
    own = [
        pltpu.make_async_copy(wuk.at[:, lanes(x, width)], wkb.at[z, x, c], loc.at[0]),
        pltpu.make_async_copy(wuv.at[:, lanes(x, width)], wvb.at[z, x, c], loc.at[1]),
        pltpu.make_async_copy(q.at[:, lanes(group, q_width)], qb.at[me], loc.at[2]),
    ]

    for copy in early:
        copy.start()
    barrier = pltpu.get_barrier_semaphore()
    for device in peers + [sib]:
        pl.semaphore_signal(barrier, inc=1, device_id=device, device_id_type=MESH)

    @pl.when(has_up)
    def _():
        pl.semaphore_signal(barrier, inc=1, device_id=up, device_id_type=MESH)

    @pl.when(has_down)
    def _():
        pl.semaphore_signal(barrier, inc=1, device_id=down, device_id_type=MESH)

    for copy in own:
        copy.start()
    for copy in early:
        copy.wait()
    own_tab = span_table(coarse[span[ctx * 2 + f]], fine[...])
    kb[z, x, c, f, :, LATENT:] = turn(kb[z, x, c, f, :, LATENT:], *own_tab)

    pl.semaphore_wait(barrier, 4 + lax.min(z, 1) + lax.min(depth - 1 - z, 1))

    def k_up(zi):
        block = kb.at[zi, x, c, f]
        return rc(block, block, ks.at[zi, 0], kr.at[zi, 0], up)

    def k_down(zi):
        block = kb.at[zi, x, c, f]
        return rc(block, block, ks.at[zi, 1], kr.at[zi, 0], down)

    def k_plane(zi, kind):
        block = kb.at[zi, x, c, f]
        return rc(block, block, ks.at[zi, 2 + kind], kr.at[zi, 1 + kind], peers[kind])

    def k_plane_in(zi, kind):
        block = kb.at[zi, plane[kind][0], c, plane[kind][1]]
        return rc(block, block, ks.at[zi, 2 + kind], kr.at[zi, 1 + kind], peers[kind])

    def k_sib(col, core):
        block = kb.at[:, cols[col][0], core, cols[col][1]]
        return rc(block, block, sks.at[col], skr.at[col], sib)

    sources = (wuk, wuv)
    bufs = (wkb, wvb)

    def w_x(m):
        return rc(
            sources[m].at[:, lanes(1 - x, width)], bufs[m].at[z, x, c], wxs.at[m], wxr.at[m], peers[0]
        )

    def w_up(m, zi):
        block = bufs[m].at[zi, :, c]
        return rc(block, block, wzs.at[m, zi, 0], wr.at[m, zi], up)

    def w_down(m, zi):
        block = bufs[m].at[zi, :, c]
        return rc(block, block, wzs.at[m, zi, 1], wr.at[m, zi], down)

    def w_sib(m, zi, core):
        block = bufs[m].at[zi, :, core]
        return rc(block, block, wss.at[m, zi], wsr.at[m, zi], sib)

    def q_send(kind):
        px, pf = plane[kind]
        return rc(
            q.at[:, lanes(pf * 2 + px, q_width)], qb.at[me], qs.at[kind], qr.at[kind], peers[kind]
        )

    def q_in(kind):
        px, pf = plane[kind]
        block = qb.at[px * 2 + pf]
        return rc(block, block, qs.at[kind], qr.at[kind], peers[kind])

    def each_round(step, on_low, on_high):
        pl.when(z - step >= 0)(lambda: on_low(z - step))
        pl.when(z + step < depth)(lambda: on_high(z + step))

    def k_low(zi):
        k_up(zi).wait_recv()
        pl.when(has_up)(lambda: k_up(zi).start())
        for kind in range(3):
            k_plane(zi, kind).start()

    def k_high(zi):
        k_down(zi).wait_recv()
        pl.when(has_down)(lambda: k_down(zi).start())
        for kind in range(3):
            k_plane(zi, kind).start()

    def w_low(m, zi):
        w_up(m, zi).wait_recv()
        pl.when(has_up)(lambda: w_up(m, zi).start())
        w_sib(m, zi, c).start()

    def w_high(m, zi):
        w_down(m, zi).wait_recv()
        pl.when(has_down)(lambda: w_down(m, zi).start())
        w_sib(m, zi, c).start()

    def k_round(step):
        each_round(step, k_low, k_high)

    def w_round(m, step):
        each_round(step, functools.partial(w_low, m), functools.partial(w_high, m))

    def w_first(m):
        rc(bufs[m].at[z, 1 - x, c], bufs[m].at[z, 1 - x, c], wxs.at[m], wxr.at[m], peers[0]).wait_recv()
        pl.when(has_up)(lambda: w_up(m, z).start())
        pl.when(has_down)(lambda: w_down(m, z).start())
        w_sib(m, z, c).start()

    w_x(0).start()
    pl.when(has_up)(lambda: k_up(z).start())
    pl.when(has_down)(lambda: k_down(z).start())
    for kind in range(3):
        k_plane(z, kind).start()
    w_x(1).start()
    for kind in range(3):
        q_send(kind).start()
    for copy in own:
        copy.wait()
    w_first(0)
    k_round(1)
    w_round(0, 1)
    w_first(1)
    for step in range(2, depth):
        k_round(step)
        w_round(0, step)
    k_sib(0, c).start()
    for kind in range(3):
        for zi in range(depth):
            k_plane_in(zi, kind).wait_recv()
        k_sib(1 + kind, c).start()
    w_round(1, 1)
    for kind in range(3):
        q_in(kind).wait_recv()
    for zi in range(depth):
        w_sib(0, zi, 1 - c).wait_recv()

    rows = 4 * SPAN
    tables = []
    places = []
    for px in range(2):
        for pf in range(2):
            held = span[((z * 2 + px) * 2 + c) * 2 + pf]
            tables.append(span_table(coarse[held], fine[...]))
            places.append(held * SPAN + lax.broadcasted_iota(jnp.int32, (SPAN, 1), 0))
    table = [jnp.concatenate(part, axis=0) for part in zip(*tables)]
    query_pos = jnp.concatenate(places, axis=0)
    queries = qb[...].reshape(rows, q_width)
    key_map = wkb[...].reshape(LATENT, width)
    lat, rot = [], []
    for head in range(heads):
        begin = head * (NOPE + ROPE)
        lat.append(
            lax.dot_general(
                queries[:, begin : begin + NOPE],
                key_map[:, head * NOPE : (head + 1) * NOPE],
                (((1,), (1,)), ((), ())),
                preferred_element_type=jnp.float32,
            ).astype(jnp.bfloat16)
        )
        rot.append(turn(queries[:, begin + NOPE : begin + NOPE + ROPE], *table))
    total_keys = depth * 8 * SPAN
    lane = lax.broadcasted_iota(jnp.int32, (1, total_keys), 1)
    key_pos = jnp.zeros((1, total_keys), jnp.int32)
    for slot in range(depth * 8):
        key_pos = jnp.where(lane // SPAN == slot, span[slot] * SPAN, key_pos)
    key_pos = key_pos + lane % SPAN
    allowed = key_pos <= query_pos

    for step in range(2, depth):
        w_round(1, step)
    for col in range(4):
        k_sib(col, 1 - c).wait_recv()

    keys_lat = kb[:, :, :, :, :, :LATENT].reshape(total_keys, LATENT)
    keys_rot = kb[:, :, :, :, :, LATENT:].reshape(total_keys, ROPE)
    scale = 1.0 / math.sqrt(NOPE + ROPE)
    outs = []
    for pair in range(2):
        pick = slice(2 * pair, 2 * pair + 2)
        score = lax.dot_general(
            jnp.concatenate(lat[pick], axis=0), keys_lat,
            (((1,), (1,)), ((), ())), preferred_element_type=jnp.float32,
        ) + lax.dot_general(
            jnp.concatenate(rot[pick], axis=0), keys_rot,
            (((1,), (1,)), ((), ())), preferred_element_type=jnp.float32,
        )
        score = jnp.where(
            allowed[None], score.reshape(2, rows, total_keys) * scale, jnp.float32(-1e30)
        ).reshape(2 * rows, total_keys)
        expo = jnp.exp(score - jnp.max(score, axis=1, keepdims=True))
        totals = jnp.sum(expo, axis=1, keepdims=True)
        accum = jnp.dot(expo.astype(jnp.bfloat16), keys_lat, preferred_element_type=jnp.float32)
        outs.append((accum * (1.0 / totals)).astype(jnp.bfloat16))

    for zi in range(depth):
        w_sib(1, zi, 1 - c).wait_recv()

    value_map = wvb[...].reshape(LATENT, width)
    for head in range(heads):
        part = outs[head // 2][(head % 2) * rows : (head % 2 + 1) * rows]
        ob[:, :, head * VDIM : (head + 1) * VDIM] = (
            jnp.dot(
                part, value_map[:, head * VDIM : (head + 1) * VDIM],
                preferred_element_type=jnp.float32,
            )
            .astype(jnp.bfloat16)
            .reshape(4, SPAN, VDIM)
        )

    def o_send(kind):
        px, pf = plane[kind]
        return rc(
            ob.at[px * 2 + pf], out.at[:, lanes(group, width)], os_.at[kind], or_.at[kind], peers[kind]
        )

    def o_in(kind):
        px, pf = plane[kind]
        block = out.at[:, lanes(pf * 2 + px, width)]
        return rc(block, block, os_.at[kind], or_.at[kind], peers[kind])

    for kind in range(3):
        o_send(kind).start()
    mine = pltpu.make_async_copy(ob.at[me], out.at[:, lanes(group, width)], loc.at[0])
    mine.start()

    for zi in range(depth):
        pl.when(jnp.logical_and(has_up, zi <= z))(lambda zi=zi: k_up(zi).wait_send())
        pl.when(jnp.logical_and(has_down, zi >= z))(lambda zi=zi: k_down(zi).wait_send())
        for kind in range(3):
            k_plane(zi, kind).wait_send()
        for m in range(2):
            pl.when(jnp.logical_and(has_up, zi <= z))(lambda zi=zi, m=m: w_up(m, zi).wait_send())
            pl.when(jnp.logical_and(has_down, zi >= z))(lambda zi=zi, m=m: w_down(m, zi).wait_send())
            w_sib(m, zi, c).wait_send()
    for m in range(2):
        w_x(m).wait_send()
    for col in range(4):
        k_sib(col, c).wait_send()
    for kind in range(3):
        q_send(kind).wait_send()
    mine.wait()
    for kind in range(3):
        o_in(kind).wait_recv()
        o_send(kind).wait_send()


def planned(query_heads, kv_latent, w_uk, w_uv, span_order):
    depth = lax.axis_size("ctx") // 4
    local_count = kv_latent.shape[0]
    width = w_uk.shape[1] // 2
    q_width = query_heads.shape[1] // 4
    dma = pltpu.SemaphoreType.DMA
    vmem = pl.BlockSpec(memory_space=pltpu.VMEM)
    spans = span_order.shape[0]
    hbm = pl.BlockSpec(memory_space=pltpu.HBM)
    coarse = jnp.asarray(rope_table(spans, SPAN).reshape(spans, 1, 2 * ROPE))
    fine = jnp.asarray(rope_table(SPAN, 1))
    return pl.pallas_call(
        kernel,
        out_shape=jax.ShapeDtypeStruct((local_count, width * 4), jnp.bfloat16),
        in_specs=[hbm] * 7,
        out_specs=vmem,
        scratch_shapes=[
            pltpu.SMEM((spans,), jnp.int32),
            pltpu.VMEM((spans, 1, 2 * ROPE), jnp.float32),
            pltpu.VMEM((SPAN, 2 * ROPE), jnp.float32),
            pltpu.VMEM((4, SPAN, q_width), jnp.bfloat16),
            pltpu.VMEM((depth, 2, 2, 2, SPAN, LATENT + ROPE), jnp.bfloat16),
            pltpu.VMEM((depth, 2, 2, w_uk.shape[0], width), jnp.bfloat16),
            pltpu.VMEM((depth, 2, 2, w_uk.shape[0], width), jnp.bfloat16),
            pltpu.VMEM((4, SPAN, width), jnp.bfloat16),
            dma((7,)),
            dma((depth, 5)), dma((depth, 4)), dma((4,)), dma((4,)),
            dma((2,)), dma((2,)), dma((2, depth, 2)), dma((2, depth)), dma((2, depth)), dma((2, depth)),
            dma((3,)), dma((3,)), dma((3,)), dma((3,)),
        ],
        compiler_params=pltpu.CompilerParams(
            collective_id=0, has_side_effects=True, vmem_limit_bytes=60 * 1024 * 1024
        ),
        name="mla_prefill",
    )(span_order, query_heads, kv_latent, w_uk, w_uv, coarse, fine)


def solution(mesh):
    placed = (
        P(("ctx", "fsdp"), None),
        P(("ctx", "fsdp"), None),
        P("ctx", "fsdp"),
        P("ctx", "fsdp"),
        P(),
    )
    small = mesh.shape["fsdp"] == 2 and mesh.shape["ctx"] == 16

    def program(query_heads, kv_latent, w_uk, w_uv, span_order):
        fits = (
            small
            and query_heads.shape[1] == 16 * (NOPE + ROPE)
            and query_heads.shape[0] == 32 * SPAN
        )
        return jax.shard_map(
            planned if fits else body,
            mesh=mesh, in_specs=placed, out_specs=P(("ctx", "fsdp"), None), check_vma=False,
        )(query_heads, kv_latent, w_uk, w_uv, span_order)

    return program
```

```python
import functools
import math

import jax
import jax.numpy as jnp
import numpy as np
from jax import lax
from jax.experimental import pallas as pl
from jax.experimental.pallas import tpu as pltpu
from jax.sharding import PartitionSpec as P

LATENT = 512
ROPE = 64
NOPE = 128
VDIM = 128
SPAN = 32


def lookup(entries, wanted):
    matches = wanted[:, None] == jnp.arange(entries.shape[0], dtype=jnp.int32)[None, :]
    return jnp.sum(jnp.where(matches, entries[None, :], 0), axis=1)


def position(span_order, row_ids):
    return lookup(span_order, row_ids // SPAN) * SPAN + row_ids % SPAN


def rotary_tables(position_ids):
    half_width = ROPE // 2
    frequency = 10000.0 ** (-jnp.arange(half_width, dtype=jnp.float32) / half_width)
    angles = position_ids.astype(jnp.float32)[:, None] * frequency[None, :]
    return (jnp.cos(angles), jnp.sin(angles))


def rotate(values, cos_table, sin_table):
    half_width = ROPE // 2
    values = values.astype(jnp.float32)
    first_half = values[..., :half_width]
    second_half = values[..., half_width:]
    turned = jnp.concatenate(
        [
            first_half * cos_table - second_half * sin_table,
            second_half * cos_table + first_half * sin_table,
        ],
        axis=-1,
    )
    return turned.astype(jnp.bfloat16)


def body(query_heads, kv_latent, w_uk, w_uv, span_order):
    ctx_index = lax.axis_index("ctx")
    fsdp_index = lax.axis_index("fsdp")
    fsdp_count = lax.axis_size("fsdp")
    local_count = kv_latent.shape[0]
    row_count = local_count * fsdp_count
    score_scale = 1.0 / math.sqrt(NOPE + ROPE)
    queries = lax.all_to_all(query_heads, "fsdp", split_axis=1, concat_axis=0, tiled=True)
    head_count = queries.shape[1] // (NOPE + ROPE)
    queries = queries.reshape(row_count, head_count, NOPE + ROPE)
    key_map, value_map = (
        lax.all_gather(w_uk, "ctx", axis=0, tiled=True),
        lax.all_gather(w_uv, "ctx", axis=0, tiled=True),
    )
    query_pos = position(span_order, ctx_index * row_count + jnp.arange(row_count, dtype=jnp.int32))
    own_ids = (
        ctx_index * row_count + fsdp_index * local_count + jnp.arange(local_count, dtype=jnp.int32)
    )
    own_cos, own_sin = rotary_tables(position(span_order, own_ids))
    local_keys = jnp.concatenate(
        [kv_latent[:, :LATENT], rotate(kv_latent[:, LATENT:], own_cos, own_sin)], axis=1
    )
    query_cos, query_sin = rotary_tables(query_pos)
    query_latent = jnp.einsum(
        "rhd,nhd->rhn",
        queries[:, :, :NOPE],
        key_map.reshape(LATENT, head_count, NOPE),
        preferred_element_type=jnp.float32,
    ).astype(jnp.bfloat16)
    query_rope = rotate(queries[:, :, NOPE:], query_cos[:, None, :], query_sin[:, None, :])
    query_full = jnp.concatenate([query_latent, query_rope], axis=2)
    segment = lax.all_gather(local_keys, ("ctx", "fsdp"), axis=0, tiled=True)
    key_pos = position(span_order, jnp.arange(segment.shape[0], dtype=jnp.int32))
    row_max = jnp.full((row_count, head_count), -1e30, jnp.float32)
    totals = jnp.zeros((row_count, head_count), jnp.float32)
    accum = jnp.zeros((row_count, head_count, LATENT), jnp.float32)
    seg_count = segment.shape[0]
    for sub_begin in range(0, seg_count, 1024):
        sub_keys = segment[sub_begin : sub_begin + 1024]
        sub_pos = key_pos[sub_begin : sub_begin + 1024]
        allowed = (sub_pos[None, :] <= query_pos[:, None])[:, None, :]
        score_block = (
            jnp.einsum("rhe,ke->rhk", query_full, sub_keys, preferred_element_type=jnp.float32)
            * score_scale
        )
        score_block = jnp.where(allowed, score_block, jnp.float32(-1e30))
        new_max = jnp.maximum(row_max, jnp.max(score_block, axis=2))
        exp_vals = jnp.where(allowed, jnp.exp(score_block - new_max[:, :, None]), jnp.float32(0.0))
        rescale = jnp.exp(row_max - new_max)
        totals = totals * rescale + jnp.sum(exp_vals, axis=2)
        accum = accum * rescale[:, :, None] + jnp.einsum(
            "rhk,kn->rhn",
            exp_vals.astype(jnp.bfloat16),
            sub_keys[:, :LATENT],
            preferred_element_type=jnp.float32,
        )
        row_max = new_max
    row_max, totals, accum = (row_max, totals, accum)
    out_latent = (accum / totals[:, :, None]).astype(jnp.bfloat16)
    head_out = jnp.einsum(
        "rhn,nhd->rhd",
        out_latent,
        value_map.reshape(LATENT, head_count, VDIM),
        preferred_element_type=jnp.float32,
    ).astype(jnp.bfloat16)
    head_out = head_out.reshape(row_count, head_count * VDIM)
    return lax.all_to_all(head_out, "fsdp", split_axis=0, concat_axis=1, tiled=True)


MESH = pl.DeviceIdType.MESH


def rope_table(count, stride):
    half_width = ROPE // 2
    frequency = 10000.0 ** (-np.arange(half_width, dtype=np.float64) / half_width)
    angles = np.arange(count)[:, None] * stride * frequency[None, :]
    cos, sin = np.cos(angles), np.sin(angles)
    return np.concatenate([cos, cos, sin, sin], axis=1).astype(np.float32)


def span_table(coarse, fine):
    cos = coarse[:, :ROPE] * fine[:, :ROPE] - coarse[:, ROPE:] * fine[:, ROPE:]
    sin = coarse[:, ROPE:] * fine[:, :ROPE] + coarse[:, :ROPE] * fine[:, ROPE:]
    first = lax.broadcasted_iota(jnp.int32, sin.shape, 1) < ROPE // 2
    return cos, jnp.where(first, -sin, sin)


def turn(values, cos, sin):
    half_width = ROPE // 2
    values = values.astype(jnp.float32)
    swapped = jnp.concatenate([values[:, half_width:], values[:, :half_width]], axis=1)
    return (values * cos + swapped * sin).astype(jnp.bfloat16)


def kernel(
    span_hbm, q, kv, wuk, wuv, coarse_hbm, fine_hbm, out,
    span, coarse, fine, qb, kb, wkb, wvb, ob,
    loc, ks, kr, sks, skr, wxs, wxr, wzs, wr, wss, wsr, qs, qr, os_, or_,
):
    depth = kb.shape[0]
    heads = 4
    width = heads * NOPE
    q_width = heads * (NOPE + ROPE)
    ctx = lax.axis_index("ctx")
    f = lax.axis_index("fsdp")
    c = lax.rem(ctx, 2)
    x = lax.rem(lax.div(ctx, 2), 2)
    z = lax.div(ctx, 4)

    def dev(z_, x_, c_, f_):
        return ((z_ * 2 + x_) * 2 + c_, f_)

    plane = [(1 - x, f), (x, 1 - f), (1 - x, 1 - f)]
    peers = [dev(z, px, c, pf) for px, pf in plane]
    sib = dev(z, x, 1 - c, f)
    up = dev(z + 1, x, c, f)
    down = dev(z - 1, x, c, f)
    has_up = z < depth - 1
    has_down = z > 0

    def rc(src, dst, ssem, rsem, device):
        return pltpu.make_async_remote_copy(
            src_ref=src, dst_ref=dst, send_sem=ssem, recv_sem=rsem,
            device_id=device, device_id_type=MESH,
        )

    def lanes(index, size):
        return pl.ds(pl.multiple_of(index * size, 128), size)

    group = f * 2 + x
    me = x * 2 + f
    early = [
        pltpu.make_async_copy(kv, kb.at[z, x, c, f], loc.at[3]),
        pltpu.make_async_copy(span_hbm, span, loc.at[4]),
        pltpu.make_async_copy(coarse_hbm, coarse, loc.at[5]),
        pltpu.make_async_copy(fine_hbm, fine, loc.at[6]),
    ]
    own = [
        pltpu.make_async_copy(wuk.at[:, lanes(x, width)], wkb.at[z, x, c], loc.at[0]),
        pltpu.make_async_copy(wuv.at[:, lanes(x, width)], wvb.at[z, x, c], loc.at[1]),
        pltpu.make_async_copy(q.at[:, lanes(group, q_width)], qb.at[me], loc.at[2]),
    ]

    for copy in early:
        copy.start()
    barrier = pltpu.get_barrier_semaphore()
    for device in peers + [sib]:
        pl.semaphore_signal(barrier, inc=1, device_id=device, device_id_type=MESH)

    @pl.when(has_up)
    def _():
        pl.semaphore_signal(barrier, inc=1, device_id=up, device_id_type=MESH)

    @pl.when(has_down)
    def _():
        pl.semaphore_signal(barrier, inc=1, device_id=down, device_id_type=MESH)

    for copy in own:
        copy.start()
    for copy in early:
        copy.wait()
    own_tab = span_table(coarse[span[ctx * 2 + f]], fine[...])
    kb[z, x, c, f, :, LATENT:] = turn(kb[z, x, c, f, :, LATENT:], *own_tab)

    pl.semaphore_wait(barrier, 4 + lax.min(z, 1) + lax.min(depth - 1 - z, 1))

    def k_up(zi):
        block = kb.at[zi, x, c, f]
        return rc(block, block, ks.at[zi, 0], kr.at[zi, 0], up)

    def k_down(zi):
        block = kb.at[zi, x, c, f]
        return rc(block, block, ks.at[zi, 1], kr.at[zi, 0], down)

    def k_plane(zi, kind):
        block = kb.at[zi, x, c, f]
        return rc(block, block, ks.at[zi, 2 + kind], kr.at[zi, 1 + kind], peers[kind])

    def k_plane_in(zi, kind):
        block = kb.at[zi, plane[kind][0], c, plane[kind][1]]
        return rc(block, block, ks.at[zi, 2 + kind], kr.at[zi, 1 + kind], peers[kind])

    def k_sib(zi, core):
        block = kb.at[zi, :, core]
        return rc(block, block, sks.at[zi], skr.at[zi], sib)

    sources = (wuk, wuv)
    bufs = (wkb, wvb)

    def w_x(m):
        return rc(
            sources[m].at[:, lanes(1 - x, width)], bufs[m].at[z, x, c], wxs.at[m], wxr.at[m], peers[0]
        )

    halves = (x, 1 - x)

    def w_up(m, half, zi):
        block = bufs[m].at[zi, halves[half], c]
        return rc(block, block, wzs.at[m, half, zi, 0], wr.at[m, half, zi], up)

    def w_down(m, half, zi):
        block = bufs[m].at[zi, halves[half], c]
        return rc(block, block, wzs.at[m, half, zi, 1], wr.at[m, half, zi], down)

    def w_sib(m, zi, core):
        block = bufs[m].at[zi, :, core]
        return rc(block, block, wss.at[m, zi], wsr.at[m, zi], sib)

    def q_send(kind):
        px, pf = plane[kind]
        return rc(
            q.at[:, lanes(pf * 2 + px, q_width)], qb.at[me], qs.at[kind], qr.at[kind], peers[kind]
        )

    def q_in(kind):
        px, pf = plane[kind]
        block = qb.at[px * 2 + pf]
        return rc(block, block, qs.at[kind], qr.at[kind], peers[kind])

    def each_round(step, on_low, on_high):
        pl.when(z - step >= 0)(lambda: on_low(z - step))
        pl.when(z + step < depth)(lambda: on_high(z + step))

    def k_low(zi):
        k_up(zi).wait_recv()
        pl.when(has_up)(lambda: k_up(zi).start())
        for kind in range(3):
            k_plane(zi, kind).start()

    def k_high(zi):
        k_down(zi).wait_recv()
        pl.when(has_down)(lambda: k_down(zi).start())
        for kind in range(3):
            k_plane(zi, kind).start()

    def w_low(m, half, zi):
        w_up(m, half, zi).wait_recv()
        pl.when(has_up)(lambda: w_up(m, half, zi).start())
        if half:
            w_sib(m, zi, c).start()

    def w_high(m, half, zi):
        w_down(m, half, zi).wait_recv()
        pl.when(has_down)(lambda: w_down(m, half, zi).start())
        if half:
            w_sib(m, zi, c).start()

    def k_plane_done(zi):
        for kind in range(3):
            k_plane_in(zi, kind).wait_recv()
        k_sib(zi, c).start()

    def w_first(m, half):
        if half:
            block = bufs[m].at[z, 1 - x, c]
            rc(block, block, wxs.at[m], wxr.at[m], peers[0]).wait_recv()
            w_sib(m, z, c).start()
        pl.when(has_up)(lambda: w_up(m, half, z).start())
        pl.when(has_down)(lambda: w_down(m, half, z).start())

    order = [(0, 0), (1, 0), (0, 1), (1, 1)]
    w_x(0).start()
    pl.when(has_up)(lambda: k_up(z).start())
    pl.when(has_down)(lambda: k_down(z).start())
    k_plane(z, 1).start()
    w_x(1).start()
    for copy in own:
        copy.wait()
    w_first(0, 0)
    w_first(1, 0)
    q_send(1).start()
    w_first(0, 1)
    k_plane(z, 0).start()
    k_plane(z, 2).start()
    w_first(1, 1)
    q_send(0).start()
    q_send(2).start()
    for step in range(1, depth):
        each_round(step, k_low, k_high)
        for m, half in order:
            each_round(
                step, functools.partial(w_low, m, half), functools.partial(w_high, m, half)
            )
        if step == 1:
            k_plane_done(z)
        else:
            each_round(step - 1, k_plane_done, k_plane_done)
    for kind in range(3):
        q_in(kind).wait_recv()
    for zi in range(depth):
        w_sib(0, zi, 1 - c).wait_recv()

    rows = 4 * SPAN
    tables = []
    places = []
    for px in range(2):
        for pf in range(2):
            held = span[((z * 2 + px) * 2 + c) * 2 + pf]
            tables.append(span_table(coarse[held], fine[...]))
            places.append(held * SPAN + lax.broadcasted_iota(jnp.int32, (SPAN, 1), 0))
    table = [jnp.concatenate(part, axis=0) for part in zip(*tables)]
    query_pos = jnp.concatenate(places, axis=0)
    queries = qb[...].reshape(rows, q_width)
    key_map = wkb[...].reshape(LATENT, width)
    lat, rot = [], []
    for head in range(heads):
        begin = head * (NOPE + ROPE)
        lat.append(
            lax.dot_general(
                queries[:, begin : begin + NOPE],
                key_map[:, head * NOPE : (head + 1) * NOPE],
                (((1,), (1,)), ((), ())),
                preferred_element_type=jnp.float32,
            ).astype(jnp.bfloat16)
        )
        rot.append(turn(queries[:, begin + NOPE : begin + NOPE + ROPE], *table))
    total_keys = depth * 8 * SPAN
    lane = lax.broadcasted_iota(jnp.int32, (1, total_keys), 1)
    key_pos = jnp.zeros((1, total_keys), jnp.int32)
    for slot in range(depth * 8):
        key_pos = jnp.where(lane // SPAN == slot, span[slot] * SPAN, key_pos)
    key_pos = key_pos + lane % SPAN
    allowed = key_pos <= query_pos

    each_round(depth - 1, k_plane_done, k_plane_done)
    for zi in range(depth):
        k_sib(zi, 1 - c).wait_recv()

    keys_lat = kb[:, :, :, :, :, :LATENT].reshape(total_keys, LATENT)
    keys_rot = kb[:, :, :, :, :, LATENT:].reshape(total_keys, ROPE)
    scale = 1.0 / math.sqrt(NOPE + ROPE)
    outs = []
    for pair in range(2):
        pick = slice(2 * pair, 2 * pair + 2)
        score = lax.dot_general(
            jnp.concatenate(lat[pick], axis=0), keys_lat,
            (((1,), (1,)), ((), ())), preferred_element_type=jnp.float32,
        ) + lax.dot_general(
            jnp.concatenate(rot[pick], axis=0), keys_rot,
            (((1,), (1,)), ((), ())), preferred_element_type=jnp.float32,
        )
        score = jnp.where(
            allowed[None], score.reshape(2, rows, total_keys) * scale, jnp.float32(-1e30)
        ).reshape(2 * rows, total_keys)
        expo = jnp.exp(score - jnp.max(score, axis=1, keepdims=True))
        totals = jnp.sum(expo, axis=1, keepdims=True)
        accum = jnp.dot(expo.astype(jnp.bfloat16), keys_lat, preferred_element_type=jnp.float32)
        outs.append((accum * (1.0 / totals)).astype(jnp.bfloat16))

    for zi in range(depth):
        w_sib(1, zi, 1 - c).wait_recv()

    value_map = wvb[...].reshape(LATENT, width)
    for head in range(heads):
        part = outs[head // 2][(head % 2) * rows : (head % 2 + 1) * rows]
        ob[:, :, head * VDIM : (head + 1) * VDIM] = (
            jnp.dot(
                part, value_map[:, head * VDIM : (head + 1) * VDIM],
                preferred_element_type=jnp.float32,
            )
            .astype(jnp.bfloat16)
            .reshape(4, SPAN, VDIM)
        )

    def o_send(kind):
        px, pf = plane[kind]
        return rc(
            ob.at[px * 2 + pf], out.at[:, lanes(group, width)], os_.at[kind], or_.at[kind], peers[kind]
        )

    def o_in(kind):
        px, pf = plane[kind]
        block = out.at[:, lanes(pf * 2 + px, width)]
        return rc(block, block, os_.at[kind], or_.at[kind], peers[kind])

    for kind in range(3):
        o_send(kind).start()
    mine = pltpu.make_async_copy(ob.at[me], out.at[:, lanes(group, width)], loc.at[0])
    mine.start()

    for zi in range(depth):
        pl.when(jnp.logical_and(has_up, zi <= z))(lambda zi=zi: k_up(zi).wait_send())
        pl.when(jnp.logical_and(has_down, zi >= z))(lambda zi=zi: k_down(zi).wait_send())
        for kind in range(3):
            k_plane(zi, kind).wait_send()
        for m in range(2):
            for half in range(2):
                pl.when(jnp.logical_and(has_up, zi <= z))(
                    lambda zi=zi, m=m, half=half: w_up(m, half, zi).wait_send()
                )
                pl.when(jnp.logical_and(has_down, zi >= z))(
                    lambda zi=zi, m=m, half=half: w_down(m, half, zi).wait_send()
                )
            w_sib(m, zi, c).wait_send()
    for m in range(2):
        w_x(m).wait_send()
    for zi in range(depth):
        k_sib(zi, c).wait_send()
    for kind in range(3):
        q_send(kind).wait_send()
    mine.wait()
    for kind in range(3):
        o_in(kind).wait_recv()
        o_send(kind).wait_send()


def planned(query_heads, kv_latent, w_uk, w_uv, span_order):
    depth = lax.axis_size("ctx") // 4
    local_count = kv_latent.shape[0]
    width = w_uk.shape[1] // 2
    q_width = query_heads.shape[1] // 4
    dma = pltpu.SemaphoreType.DMA
    vmem = pl.BlockSpec(memory_space=pltpu.VMEM)
    spans = span_order.shape[0]
    hbm = pl.BlockSpec(memory_space=pltpu.HBM)
    coarse = jnp.asarray(rope_table(spans, SPAN).reshape(spans, 1, 2 * ROPE))
    fine = jnp.asarray(rope_table(SPAN, 1))
    return pl.pallas_call(
        kernel,
        out_shape=jax.ShapeDtypeStruct((local_count, width * 4), jnp.bfloat16),
        in_specs=[hbm] * 7,
        out_specs=vmem,
        scratch_shapes=[
            pltpu.SMEM((spans,), jnp.int32),
            pltpu.VMEM((spans, 1, 2 * ROPE), jnp.float32),
            pltpu.VMEM((SPAN, 2 * ROPE), jnp.float32),
            pltpu.VMEM((4, SPAN, q_width), jnp.bfloat16),
            pltpu.VMEM((depth, 2, 2, 2, SPAN, LATENT + ROPE), jnp.bfloat16),
            pltpu.VMEM((depth, 2, 2, w_uk.shape[0], width), jnp.bfloat16),
            pltpu.VMEM((depth, 2, 2, w_uk.shape[0], width), jnp.bfloat16),
            pltpu.VMEM((4, SPAN, width), jnp.bfloat16),
            dma((7,)),
            dma((depth, 5)), dma((depth, 4)), dma((depth,)), dma((depth,)),
            dma((2,)), dma((2,)), dma((2, 2, depth, 2)), dma((2, 2, depth)), dma((2, depth)), dma((2, depth)),
            dma((3,)), dma((3,)), dma((3,)), dma((3,)),
        ],
        compiler_params=pltpu.CompilerParams(
            collective_id=0, has_side_effects=True, vmem_limit_bytes=60 * 1024 * 1024
        ),
        name="mla_prefill",
    )(span_order, query_heads, kv_latent, w_uk, w_uv, coarse, fine)


def solution(mesh):
    placed = (
        P(("ctx", "fsdp"), None),
        P(("ctx", "fsdp"), None),
        P("ctx", "fsdp"),
        P("ctx", "fsdp"),
        P(),
    )
    small = mesh.shape["fsdp"] == 2 and mesh.shape["ctx"] == 16

    def program(query_heads, kv_latent, w_uk, w_uv, span_order):
        fits = (
            small
            and query_heads.shape[1] == 16 * (NOPE + ROPE)
            and query_heads.shape[0] == 32 * SPAN
        )
        return jax.shard_map(
            planned if fits else body,
            mesh=mesh, in_specs=placed, out_specs=P(("ctx", "fsdp"), None), check_vma=False,
        )(query_heads, kv_latent, w_uk, w_uv, span_order)

    return program
```

```python
import functools
import math

import jax
import jax.numpy as jnp
import numpy as np
from jax import lax
from jax.experimental import pallas as pl
from jax.experimental.pallas import tpu as pltpu
from jax.sharding import PartitionSpec as P

LATENT = 512
ROPE = 64
NOPE = 128
VDIM = 128
SPAN = 32


def lookup(entries, wanted):
    matches = wanted[:, None] == jnp.arange(entries.shape[0], dtype=jnp.int32)[None, :]
    return jnp.sum(jnp.where(matches, entries[None, :], 0), axis=1)


def position(span_order, row_ids):
    return lookup(span_order, row_ids // SPAN) * SPAN + row_ids % SPAN


def rotary_tables(position_ids):
    half_width = ROPE // 2
    frequency = 10000.0 ** (-jnp.arange(half_width, dtype=jnp.float32) / half_width)
    angles = position_ids.astype(jnp.float32)[:, None] * frequency[None, :]
    return (jnp.cos(angles), jnp.sin(angles))


def rotate(values, cos_table, sin_table):
    half_width = ROPE // 2
    values = values.astype(jnp.float32)
    first_half = values[..., :half_width]
    second_half = values[..., half_width:]
    turned = jnp.concatenate(
        [
            first_half * cos_table - second_half * sin_table,
            second_half * cos_table + first_half * sin_table,
        ],
        axis=-1,
    )
    return turned.astype(jnp.bfloat16)


def body(query_heads, kv_latent, w_uk, w_uv, span_order):
    ctx_index = lax.axis_index("ctx")
    fsdp_index = lax.axis_index("fsdp")
    fsdp_count = lax.axis_size("fsdp")
    local_count = kv_latent.shape[0]
    row_count = local_count * fsdp_count
    score_scale = 1.0 / math.sqrt(NOPE + ROPE)
    queries = lax.all_to_all(query_heads, "fsdp", split_axis=1, concat_axis=0, tiled=True)
    head_count = queries.shape[1] // (NOPE + ROPE)
    queries = queries.reshape(row_count, head_count, NOPE + ROPE)
    key_map, value_map = (
        lax.all_gather(w_uk, "ctx", axis=0, tiled=True),
        lax.all_gather(w_uv, "ctx", axis=0, tiled=True),
    )
    query_pos = position(span_order, ctx_index * row_count + jnp.arange(row_count, dtype=jnp.int32))
    own_ids = (
        ctx_index * row_count + fsdp_index * local_count + jnp.arange(local_count, dtype=jnp.int32)
    )
    own_cos, own_sin = rotary_tables(position(span_order, own_ids))
    local_keys = jnp.concatenate(
        [kv_latent[:, :LATENT], rotate(kv_latent[:, LATENT:], own_cos, own_sin)], axis=1
    )
    query_cos, query_sin = rotary_tables(query_pos)
    query_latent = jnp.einsum(
        "rhd,nhd->rhn",
        queries[:, :, :NOPE],
        key_map.reshape(LATENT, head_count, NOPE),
        preferred_element_type=jnp.float32,
    ).astype(jnp.bfloat16)
    query_rope = rotate(queries[:, :, NOPE:], query_cos[:, None, :], query_sin[:, None, :])
    query_full = jnp.concatenate([query_latent, query_rope], axis=2)
    segment = lax.all_gather(local_keys, ("ctx", "fsdp"), axis=0, tiled=True)
    key_pos = position(span_order, jnp.arange(segment.shape[0], dtype=jnp.int32))
    row_max = jnp.full((row_count, head_count), -1e30, jnp.float32)
    totals = jnp.zeros((row_count, head_count), jnp.float32)
    accum = jnp.zeros((row_count, head_count, LATENT), jnp.float32)
    seg_count = segment.shape[0]
    for sub_begin in range(0, seg_count, 1024):
        sub_keys = segment[sub_begin : sub_begin + 1024]
        sub_pos = key_pos[sub_begin : sub_begin + 1024]
        allowed = (sub_pos[None, :] <= query_pos[:, None])[:, None, :]
        score_block = (
            jnp.einsum("rhe,ke->rhk", query_full, sub_keys, preferred_element_type=jnp.float32)
            * score_scale
        )
        score_block = jnp.where(allowed, score_block, jnp.float32(-1e30))
        new_max = jnp.maximum(row_max, jnp.max(score_block, axis=2))
        exp_vals = jnp.where(allowed, jnp.exp(score_block - new_max[:, :, None]), jnp.float32(0.0))
        rescale = jnp.exp(row_max - new_max)
        totals = totals * rescale + jnp.sum(exp_vals, axis=2)
        accum = accum * rescale[:, :, None] + jnp.einsum(
            "rhk,kn->rhn",
            exp_vals.astype(jnp.bfloat16),
            sub_keys[:, :LATENT],
            preferred_element_type=jnp.float32,
        )
        row_max = new_max
    row_max, totals, accum = (row_max, totals, accum)
    out_latent = (accum / totals[:, :, None]).astype(jnp.bfloat16)
    head_out = jnp.einsum(
        "rhn,nhd->rhd",
        out_latent,
        value_map.reshape(LATENT, head_count, VDIM),
        preferred_element_type=jnp.float32,
    ).astype(jnp.bfloat16)
    head_out = head_out.reshape(row_count, head_count * VDIM)
    return lax.all_to_all(head_out, "fsdp", split_axis=0, concat_axis=1, tiled=True)


MESH = pl.DeviceIdType.MESH


def rope_table(count, stride):
    half_width = ROPE // 2
    frequency = 10000.0 ** (-np.arange(half_width, dtype=np.float64) / half_width)
    angles = np.arange(count)[:, None] * stride * frequency[None, :]
    cos, sin = np.cos(angles), np.sin(angles)
    return np.concatenate([cos, cos, sin, sin], axis=1).astype(np.float32)


def span_table(coarse, fine):
    cos = coarse[:, :ROPE] * fine[:, :ROPE] - coarse[:, ROPE:] * fine[:, ROPE:]
    sin = coarse[:, ROPE:] * fine[:, :ROPE] + coarse[:, :ROPE] * fine[:, ROPE:]
    first = lax.broadcasted_iota(jnp.int32, sin.shape, 1) < ROPE // 2
    return cos, jnp.where(first, -sin, sin)


def turn(values, cos, sin):
    half_width = ROPE // 2
    values = values.astype(jnp.float32)
    swapped = jnp.concatenate([values[:, half_width:], values[:, :half_width]], axis=1)
    return (values * cos + swapped * sin).astype(jnp.bfloat16)


def kernel(
    span_hbm, q, kv, wuk, wuv, coarse_hbm, fine_hbm, out,
    span, coarse, fine, qb, kb, wkb, wvb, ob,
    loc, ks, kr, sks, skr, wxs, wxr, wzs, wr, wss, wsr, qs, qr, os_, or_,
):
    depth = kb.shape[0]
    heads = 4
    width = heads * NOPE
    q_width = heads * (NOPE + ROPE)
    ctx = lax.axis_index("ctx")
    f = lax.axis_index("fsdp")
    c = lax.rem(ctx, 2)
    x = lax.rem(lax.div(ctx, 2), 2)
    z = lax.div(ctx, 4)

    def dev(z_, x_, c_, f_):
        return ((z_ * 2 + x_) * 2 + c_, f_)

    plane = [(1 - x, f), (x, 1 - f), (1 - x, 1 - f)]
    peers = [dev(z, px, c, pf) for px, pf in plane]
    sib = dev(z, x, 1 - c, f)
    up = dev(z + 1, x, c, f)
    down = dev(z - 1, x, c, f)
    has_up = z < depth - 1
    has_down = z > 0

    def rc(src, dst, ssem, rsem, device):
        return pltpu.make_async_remote_copy(
            src_ref=src, dst_ref=dst, send_sem=ssem, recv_sem=rsem,
            device_id=device, device_id_type=MESH,
        )

    def lanes(index, size):
        return pl.ds(pl.multiple_of(index * size, 128), size)

    group = f * 2 + x
    me = x * 2 + f
    early = [
        pltpu.make_async_copy(kv, kb.at[z, x, c, f], loc.at[3]),
        pltpu.make_async_copy(span_hbm, span, loc.at[4]),
        pltpu.make_async_copy(coarse_hbm, coarse, loc.at[5]),
        pltpu.make_async_copy(fine_hbm, fine, loc.at[6]),
    ]
    own = [
        pltpu.make_async_copy(wuk.at[:, lanes(x, width)], wkb.at[z, x, c], loc.at[0]),
        pltpu.make_async_copy(wuv.at[:, lanes(x, width)], wvb.at[z, x, c], loc.at[1]),
        pltpu.make_async_copy(q.at[:, lanes(group, q_width)], qb.at[me], loc.at[2]),
    ]

    for copy in early:
        copy.start()
    barrier = pltpu.get_barrier_semaphore()
    for device in peers + [sib]:
        pl.semaphore_signal(barrier, inc=1, device_id=device, device_id_type=MESH)

    @pl.when(has_up)
    def _():
        pl.semaphore_signal(barrier, inc=1, device_id=up, device_id_type=MESH)

    @pl.when(has_down)
    def _():
        pl.semaphore_signal(barrier, inc=1, device_id=down, device_id_type=MESH)

    for copy in own:
        copy.start()
    for copy in early:
        copy.wait()
    own_tab = span_table(coarse[span[ctx * 2 + f]], fine[...])
    kb[z, x, c, f, :, LATENT:] = turn(kb[z, x, c, f, :, LATENT:], *own_tab)

    pl.semaphore_wait(barrier, 4 + lax.min(z, 1) + lax.min(depth - 1 - z, 1))

    def k_up(zi):
        block = kb.at[zi, x, c, f]
        return rc(block, block, ks.at[zi, 0], kr.at[zi, 0], up)

    def k_down(zi):
        block = kb.at[zi, x, c, f]
        return rc(block, block, ks.at[zi, 1], kr.at[zi, 0], down)

    def k_plane(zi, kind):
        block = kb.at[zi, x, c, f]
        return rc(block, block, ks.at[zi, 2 + kind], kr.at[zi, 1 + kind], peers[kind])

    def k_plane_in(zi, kind):
        block = kb.at[zi, plane[kind][0], c, plane[kind][1]]
        return rc(block, block, ks.at[zi, 2 + kind], kr.at[zi, 1 + kind], peers[kind])

    def k_diag(zi):
        block = kb.at[zi, 1 - x, c, f]
        return rc(block, block, ks.at[zi, 4], kr.at[zi, 3], peers[1])

    def k_diag_in(zi):
        block = kb.at[zi, 1 - x, c, 1 - f]
        return rc(block, block, ks.at[zi, 4], kr.at[zi, 3], peers[1])

    def k_sib(zi, core):
        block = kb.at[zi, :, core]
        return rc(block, block, sks.at[zi], skr.at[zi], sib)

    sources = (wuk, wuv)
    bufs = (wkb, wvb)

    def w_x(m):
        return rc(
            sources[m].at[:, lanes(1 - x, width)], bufs[m].at[z, x, c], wxs.at[m], wxr.at[m], peers[0]
        )

    halves = (x, 1 - x)

    def w_up(m, half, zi):
        block = bufs[m].at[zi, halves[half], c]
        return rc(block, block, wzs.at[m, half, zi, 0], wr.at[m, half, zi], up)

    def w_down(m, half, zi):
        block = bufs[m].at[zi, halves[half], c]
        return rc(block, block, wzs.at[m, half, zi, 1], wr.at[m, half, zi], down)

    def w_sib(m, zi, core):
        block = bufs[m].at[zi, :, core]
        return rc(block, block, wss.at[m, zi], wsr.at[m, zi], sib)

    def q_send(kind):
        px, pf = plane[kind]
        return rc(
            q.at[:, lanes(pf * 2 + px, q_width)], qb.at[me], qs.at[kind], qr.at[kind], peers[kind]
        )

    def q_in(kind):
        px, pf = plane[kind]
        block = qb.at[px * 2 + pf]
        return rc(block, block, qs.at[kind], qr.at[kind], peers[kind])

    def each_round(step, on_low, on_high):
        pl.when(z - step >= 0)(lambda: on_low(z - step))
        pl.when(z + step < depth)(lambda: on_high(z + step))

    def k_low(zi):
        k_up(zi).wait_recv()
        pl.when(has_up)(lambda: k_up(zi).start())
        for kind in range(2):
            k_plane(zi, kind).start()

    def k_high(zi):
        k_down(zi).wait_recv()
        pl.when(has_down)(lambda: k_down(zi).start())
        for kind in range(2):
            k_plane(zi, kind).start()

    def w_low(m, half, zi):
        w_up(m, half, zi).wait_recv()
        pl.when(has_up)(lambda: w_up(m, half, zi).start())
        if half:
            w_sib(m, zi, c).start()

    def w_high(m, half, zi):
        w_down(m, half, zi).wait_recv()
        pl.when(has_down)(lambda: w_down(m, half, zi).start())
        if half:
            w_sib(m, zi, c).start()

    def k_pass(zi):
        k_plane_in(zi, 0).wait_recv()
        k_diag(zi).start()

    def k_plane_done(zi):
        k_plane_in(zi, 1).wait_recv()
        k_diag_in(zi).wait_recv()
        k_sib(zi, c).start()

    def w_first(m, half):
        if half:
            block = bufs[m].at[z, 1 - x, c]
            rc(block, block, wxs.at[m], wxr.at[m], peers[0]).wait_recv()
            w_sib(m, z, c).start()
        pl.when(has_up)(lambda: w_up(m, half, z).start())
        pl.when(has_down)(lambda: w_down(m, half, z).start())

    order = [(0, 0), (1, 0), (0, 1), (1, 1)]
    w_x(0).start()
    pl.when(has_up)(lambda: k_up(z).start())
    pl.when(has_down)(lambda: k_down(z).start())
    k_plane(z, 1).start()
    w_x(1).start()
    for copy in own:
        copy.wait()
    w_first(0, 0)
    w_first(1, 0)
    q_send(1).start()
    w_first(0, 1)
    k_plane(z, 0).start()
    w_first(1, 1)
    q_send(0).start()
    q_send(2).start()
    for step in range(1, depth):
        each_round(step, k_low, k_high)
        if step == 1:
            k_pass(z)
        else:
            each_round(step - 1, k_pass, k_pass)
        for m, half in order:
            each_round(
                step, functools.partial(w_low, m, half), functools.partial(w_high, m, half)
            )
        if step == 1:
            k_plane_done(z)
        else:
            each_round(step - 1, k_plane_done, k_plane_done)
    each_round(depth - 1, k_pass, k_pass)
    for kind in range(3):
        q_in(kind).wait_recv()
    for zi in range(depth):
        w_sib(0, zi, 1 - c).wait_recv()

    rows = 4 * SPAN
    tables = []
    places = []
    for px in range(2):
        for pf in range(2):
            held = span[((z * 2 + px) * 2 + c) * 2 + pf]
            tables.append(span_table(coarse[held], fine[...]))
            places.append(held * SPAN + lax.broadcasted_iota(jnp.int32, (SPAN, 1), 0))
    table = [jnp.concatenate(part, axis=0) for part in zip(*tables)]
    query_pos = jnp.concatenate(places, axis=0)
    queries = qb[...].reshape(rows, q_width)
    key_map = wkb[...].reshape(LATENT, width)
    lat, rot = [], []
    for head in range(heads):
        begin = head * (NOPE + ROPE)
        lat.append(
            lax.dot_general(
                queries[:, begin : begin + NOPE],
                key_map[:, head * NOPE : (head + 1) * NOPE],
                (((1,), (1,)), ((), ())),
                preferred_element_type=jnp.float32,
            ).astype(jnp.bfloat16)
        )
        rot.append(turn(queries[:, begin + NOPE : begin + NOPE + ROPE], *table))
    total_keys = depth * 8 * SPAN
    lane = lax.broadcasted_iota(jnp.int32, (1, total_keys), 1)
    key_pos = jnp.zeros((1, total_keys), jnp.int32)
    for slot in range(depth * 8):
        key_pos = jnp.where(lane // SPAN == slot, span[slot] * SPAN, key_pos)
    key_pos = key_pos + lane % SPAN
    allowed = key_pos <= query_pos

    each_round(depth - 1, k_plane_done, k_plane_done)
    for zi in range(depth):
        k_sib(zi, 1 - c).wait_recv()

    keys_lat = kb[:, :, :, :, :, :LATENT].reshape(total_keys, LATENT)
    keys_rot = kb[:, :, :, :, :, LATENT:].reshape(total_keys, ROPE)
    scale = 1.0 / math.sqrt(NOPE + ROPE)
    for zi in range(depth):
        w_sib(1, zi, 1 - c).wait_recv()
    value_map = wvb[...].reshape(LATENT, width)

    def o_cols(index, pair):
        half = width // 2
        return pl.ds(pl.multiple_of(index * width + pair * half, 128), half)

    def o_send(pair, kind):
        px, pf = plane[kind]
        return rc(
            ob.at[pair, px * 2 + pf], out.at[:, o_cols(group, pair)],
            os_.at[pair, kind], or_.at[pair, kind], peers[kind],
        )

    def o_in(pair, kind):
        px, pf = plane[kind]
        block = out.at[:, o_cols(pf * 2 + px, pair)]
        return rc(block, block, os_.at[pair, kind], or_.at[pair, kind], peers[kind])

    def o_own(pair):
        return pltpu.make_async_copy(
            ob.at[pair, me], out.at[:, o_cols(group, pair)], loc.at[pair]
        )

    for pair in range(2):
        pick = slice(2 * pair, 2 * pair + 2)
        score = lax.dot_general(
            jnp.concatenate(lat[pick], axis=0), keys_lat,
            (((1,), (1,)), ((), ())), preferred_element_type=jnp.float32,
        ) + lax.dot_general(
            jnp.concatenate(rot[pick], axis=0), keys_rot,
            (((1,), (1,)), ((), ())), preferred_element_type=jnp.float32,
        )
        score = jnp.where(
            allowed[None], score.reshape(2, rows, total_keys) * scale, jnp.float32(-1e30)
        ).reshape(2 * rows, total_keys)
        expo = jnp.exp(score - jnp.max(score, axis=1, keepdims=True))
        totals = jnp.sum(expo, axis=1, keepdims=True)
        accum = jnp.dot(expo.astype(jnp.bfloat16), keys_lat, preferred_element_type=jnp.float32)
        latent = (accum * (1.0 / totals)).astype(jnp.bfloat16)
        for turn_at in range(2):
            head = 2 * pair + turn_at
            ob[pair, :, :, turn_at * VDIM : (turn_at + 1) * VDIM] = (
                jnp.dot(
                    latent[turn_at * rows : (turn_at + 1) * rows],
                    value_map[:, head * VDIM : (head + 1) * VDIM],
                    preferred_element_type=jnp.float32,
                )
                .astype(jnp.bfloat16)
                .reshape(4, SPAN, VDIM)
            )
        for kind in (2, 0, 1):
            o_send(pair, kind).start()
        o_own(pair).start()

    for zi in range(depth):
        pl.when(jnp.logical_and(has_up, zi <= z))(lambda zi=zi: k_up(zi).wait_send())
        pl.when(jnp.logical_and(has_down, zi >= z))(lambda zi=zi: k_down(zi).wait_send())
        for kind in range(2):
            k_plane(zi, kind).wait_send()
        k_diag(zi).wait_send()
        for m in range(2):
            for half in range(2):
                pl.when(jnp.logical_and(has_up, zi <= z))(
                    lambda zi=zi, m=m, half=half: w_up(m, half, zi).wait_send()
                )
                pl.when(jnp.logical_and(has_down, zi >= z))(
                    lambda zi=zi, m=m, half=half: w_down(m, half, zi).wait_send()
                )
            w_sib(m, zi, c).wait_send()
    for m in range(2):
        w_x(m).wait_send()
    for zi in range(depth):
        k_sib(zi, c).wait_send()
    for kind in range(3):
        q_send(kind).wait_send()
    for pair in range(2):
        o_own(pair).wait()
        for kind in range(3):
            o_in(pair, kind).wait_recv()
            o_send(pair, kind).wait_send()


def planned(query_heads, kv_latent, w_uk, w_uv, span_order):
    depth = lax.axis_size("ctx") // 4
    local_count = kv_latent.shape[0]
    width = w_uk.shape[1] // 2
    q_width = query_heads.shape[1] // 4
    dma = pltpu.SemaphoreType.DMA
    vmem = pl.BlockSpec(memory_space=pltpu.VMEM)
    spans = span_order.shape[0]
    hbm = pl.BlockSpec(memory_space=pltpu.HBM)
    coarse = jnp.asarray(rope_table(spans, SPAN).reshape(spans, 1, 2 * ROPE))
    fine = jnp.asarray(rope_table(SPAN, 1))
    return pl.pallas_call(
        kernel,
        out_shape=jax.ShapeDtypeStruct((local_count, width * 4), jnp.bfloat16),
        in_specs=[hbm] * 7,
        out_specs=vmem,
        scratch_shapes=[
            pltpu.SMEM((spans,), jnp.int32),
            pltpu.VMEM((spans, 1, 2 * ROPE), jnp.float32),
            pltpu.VMEM((SPAN, 2 * ROPE), jnp.float32),
            pltpu.VMEM((4, SPAN, q_width), jnp.bfloat16),
            pltpu.VMEM((depth, 2, 2, 2, SPAN, LATENT + ROPE), jnp.bfloat16),
            pltpu.VMEM((depth, 2, 2, w_uk.shape[0], width), jnp.bfloat16),
            pltpu.VMEM((depth, 2, 2, w_uk.shape[0], width), jnp.bfloat16),
            pltpu.VMEM((2, 4, SPAN, width // 2), jnp.bfloat16),
            dma((7,)),
            dma((depth, 5)), dma((depth, 4)), dma((depth,)), dma((depth,)),
            dma((2,)), dma((2,)), dma((2, 2, depth, 2)), dma((2, 2, depth)), dma((2, depth)), dma((2, depth)),
            dma((3,)), dma((3,)), dma((2, 3)), dma((2, 3)),
        ],
        compiler_params=pltpu.CompilerParams(
            collective_id=0, has_side_effects=True, vmem_limit_bytes=60 * 1024 * 1024
        ),
        name="mla_prefill",
    )(span_order, query_heads, kv_latent, w_uk, w_uv, coarse, fine)


def solution(mesh):
    placed = (
        P(("ctx", "fsdp"), None),
        P(("ctx", "fsdp"), None),
        P("ctx", "fsdp"),
        P("ctx", "fsdp"),
        P(),
    )
    small = mesh.shape["fsdp"] == 2 and mesh.shape["ctx"] == 16

    def program(query_heads, kv_latent, w_uk, w_uv, span_order):
        fits = (
            small
            and query_heads.shape[1] == 16 * (NOPE + ROPE)
            and query_heads.shape[0] == 32 * SPAN
        )
        return jax.shard_map(
            planned if fits else body,
            mesh=mesh, in_specs=placed, out_specs=P(("ctx", "fsdp"), None), check_vma=False,
        )(query_heads, kv_latent, w_uk, w_uv, span_order)

    return program
```

```python
import functools
import math

import jax
import jax.numpy as jnp
import numpy as np
from jax import lax
from jax.experimental import pallas as pl
from jax.experimental.pallas import tpu as pltpu
from jax.sharding import PartitionSpec as P

LATENT = 512
ROPE = 64
NOPE = 128
VDIM = 128
SPAN = 32


def lookup(entries, wanted):
    matches = wanted[:, None] == jnp.arange(entries.shape[0], dtype=jnp.int32)[None, :]
    return jnp.sum(jnp.where(matches, entries[None, :], 0), axis=1)


def position(span_order, row_ids):
    return lookup(span_order, row_ids // SPAN) * SPAN + row_ids % SPAN


def rotary_tables(position_ids):
    half_width = ROPE // 2
    frequency = 10000.0 ** (-jnp.arange(half_width, dtype=jnp.float32) / half_width)
    angles = position_ids.astype(jnp.float32)[:, None] * frequency[None, :]
    return (jnp.cos(angles), jnp.sin(angles))


def rotate(values, cos_table, sin_table):
    half_width = ROPE // 2
    values = values.astype(jnp.float32)
    first_half = values[..., :half_width]
    second_half = values[..., half_width:]
    turned = jnp.concatenate(
        [
            first_half * cos_table - second_half * sin_table,
            second_half * cos_table + first_half * sin_table,
        ],
        axis=-1,
    )
    return turned.astype(jnp.bfloat16)


def body(query_heads, kv_latent, w_uk, w_uv, span_order):
    ctx_index = lax.axis_index("ctx")
    fsdp_index = lax.axis_index("fsdp")
    fsdp_count = lax.axis_size("fsdp")
    local_count = kv_latent.shape[0]
    row_count = local_count * fsdp_count
    score_scale = 1.0 / math.sqrt(NOPE + ROPE)
    queries = lax.all_to_all(query_heads, "fsdp", split_axis=1, concat_axis=0, tiled=True)
    head_count = queries.shape[1] // (NOPE + ROPE)
    queries = queries.reshape(row_count, head_count, NOPE + ROPE)
    key_map, value_map = (
        lax.all_gather(w_uk, "ctx", axis=0, tiled=True),
        lax.all_gather(w_uv, "ctx", axis=0, tiled=True),
    )
    query_pos = position(span_order, ctx_index * row_count + jnp.arange(row_count, dtype=jnp.int32))
    own_ids = (
        ctx_index * row_count + fsdp_index * local_count + jnp.arange(local_count, dtype=jnp.int32)
    )
    own_cos, own_sin = rotary_tables(position(span_order, own_ids))
    local_keys = jnp.concatenate(
        [kv_latent[:, :LATENT], rotate(kv_latent[:, LATENT:], own_cos, own_sin)], axis=1
    )
    query_cos, query_sin = rotary_tables(query_pos)
    query_latent = jnp.einsum(
        "rhd,nhd->rhn",
        queries[:, :, :NOPE],
        key_map.reshape(LATENT, head_count, NOPE),
        preferred_element_type=jnp.float32,
    ).astype(jnp.bfloat16)
    query_rope = rotate(queries[:, :, NOPE:], query_cos[:, None, :], query_sin[:, None, :])
    query_full = jnp.concatenate([query_latent, query_rope], axis=2)
    segment = lax.all_gather(local_keys, ("ctx", "fsdp"), axis=0, tiled=True)
    key_pos = position(span_order, jnp.arange(segment.shape[0], dtype=jnp.int32))
    row_max = jnp.full((row_count, head_count), -1e30, jnp.float32)
    totals = jnp.zeros((row_count, head_count), jnp.float32)
    accum = jnp.zeros((row_count, head_count, LATENT), jnp.float32)
    seg_count = segment.shape[0]
    for sub_begin in range(0, seg_count, 1024):
        sub_keys = segment[sub_begin : sub_begin + 1024]
        sub_pos = key_pos[sub_begin : sub_begin + 1024]
        allowed = (sub_pos[None, :] <= query_pos[:, None])[:, None, :]
        score_block = (
            jnp.einsum("rhe,ke->rhk", query_full, sub_keys, preferred_element_type=jnp.float32)
            * score_scale
        )
        score_block = jnp.where(allowed, score_block, jnp.float32(-1e30))
        new_max = jnp.maximum(row_max, jnp.max(score_block, axis=2))
        exp_vals = jnp.where(allowed, jnp.exp(score_block - new_max[:, :, None]), jnp.float32(0.0))
        rescale = jnp.exp(row_max - new_max)
        totals = totals * rescale + jnp.sum(exp_vals, axis=2)
        accum = accum * rescale[:, :, None] + jnp.einsum(
            "rhk,kn->rhn",
            exp_vals.astype(jnp.bfloat16),
            sub_keys[:, :LATENT],
            preferred_element_type=jnp.float32,
        )
        row_max = new_max
    row_max, totals, accum = (row_max, totals, accum)
    out_latent = (accum / totals[:, :, None]).astype(jnp.bfloat16)
    head_out = jnp.einsum(
        "rhn,nhd->rhd",
        out_latent,
        value_map.reshape(LATENT, head_count, VDIM),
        preferred_element_type=jnp.float32,
    ).astype(jnp.bfloat16)
    head_out = head_out.reshape(row_count, head_count * VDIM)
    return lax.all_to_all(head_out, "fsdp", split_axis=0, concat_axis=1, tiled=True)


MESH = pl.DeviceIdType.MESH


def rope_table(count, stride):
    half_width = ROPE // 2
    frequency = 10000.0 ** (-np.arange(half_width, dtype=np.float64) / half_width)
    angles = np.arange(count)[:, None] * stride * frequency[None, :]
    cos, sin = np.cos(angles), np.sin(angles)
    return np.concatenate([cos, cos, sin, sin], axis=1).astype(np.float32)


def span_table(coarse, fine):
    cos = coarse[:, :ROPE] * fine[:, :ROPE] - coarse[:, ROPE:] * fine[:, ROPE:]
    sin = coarse[:, ROPE:] * fine[:, :ROPE] + coarse[:, :ROPE] * fine[:, ROPE:]
    first = lax.broadcasted_iota(jnp.int32, sin.shape, 1) < ROPE // 2
    return cos, jnp.where(first, -sin, sin)


def turn(values, cos, sin):
    half_width = ROPE // 2
    values = values.astype(jnp.float32)
    swapped = jnp.concatenate([values[:, half_width:], values[:, :half_width]], axis=1)
    return (values * cos + swapped * sin).astype(jnp.bfloat16)


def kernel(
    span_hbm, q, kv, wuk, wuv, coarse_hbm, fine_hbm, out,
    span, coarse, fine, qb, kb, wkb, wvb, ob,
    loc, ks, kr, sks, skr, wxs, wxr, wzs, wr, wss, wsr, qs, qr, os_, or_,
):
    depth = kb.shape[0]
    heads = 4
    width = heads * NOPE
    q_width = heads * (NOPE + ROPE)
    ctx = lax.axis_index("ctx")
    f = lax.axis_index("fsdp")
    c = lax.rem(ctx, 2)
    x = lax.rem(lax.div(ctx, 2), 2)
    z = lax.div(ctx, 4)

    def dev(z_, x_, c_, f_):
        return ((z_ * 2 + x_) * 2 + c_, f_)

    plane = [(1 - x, f), (x, 1 - f), (1 - x, 1 - f)]
    peers = [dev(z, px, c, pf) for px, pf in plane]
    sib = dev(z, x, 1 - c, f)
    up = dev(z + 1, x, c, f)
    down = dev(z - 1, x, c, f)
    has_up = z < depth - 1
    has_down = z > 0

    def rc(src, dst, ssem, rsem, device):
        return pltpu.make_async_remote_copy(
            src_ref=src, dst_ref=dst, send_sem=ssem, recv_sem=rsem,
            device_id=device, device_id_type=MESH,
        )

    def lanes(index, size):
        return pl.ds(pl.multiple_of(index * size, 128), size)

    group = f * 2 + x
    me = x * 2 + f
    early = [
        pltpu.make_async_copy(kv, kb.at[z, x, c, f], loc.at[3]),
        pltpu.make_async_copy(span_hbm, span, loc.at[4]),
        pltpu.make_async_copy(coarse_hbm, coarse, loc.at[5]),
        pltpu.make_async_copy(fine_hbm, fine, loc.at[6]),
    ]
    own = [
        pltpu.make_async_copy(wuk.at[:, lanes(x, width)], wkb.at[z, x, c], loc.at[0]),
        pltpu.make_async_copy(wuv.at[:, lanes(x, width)], wvb.at[z, x, c], loc.at[1]),
        pltpu.make_async_copy(q.at[:, lanes(group, q_width)], qb.at[me], loc.at[2]),
    ]

    for copy in early:
        copy.start()
    barrier = pltpu.get_barrier_semaphore()
    for device in peers + [sib]:
        pl.semaphore_signal(barrier, inc=1, device_id=device, device_id_type=MESH)

    @pl.when(has_up)
    def _():
        pl.semaphore_signal(barrier, inc=1, device_id=up, device_id_type=MESH)

    @pl.when(has_down)
    def _():
        pl.semaphore_signal(barrier, inc=1, device_id=down, device_id_type=MESH)

    for copy in own:
        copy.start()
    for copy in early:
        copy.wait()
    own_tab = span_table(coarse[span[ctx * 2 + f]], fine[...])
    kb[z, x, c, f, :, LATENT:] = turn(kb[z, x, c, f, :, LATENT:], *own_tab)

    pl.semaphore_wait(barrier, 4 + lax.min(z, 1) + lax.min(depth - 1 - z, 1))

    def k_up(zi):
        block = kb.at[zi, x, c, f]
        return rc(block, block, ks.at[zi, 0], kr.at[zi, 0], up)

    def k_down(zi):
        block = kb.at[zi, x, c, f]
        return rc(block, block, ks.at[zi, 1], kr.at[zi, 0], down)

    def k_plane(zi, kind):
        block = kb.at[zi, x, c, f]
        return rc(block, block, ks.at[zi, 2 + kind], kr.at[zi, 1 + kind], peers[kind])

    def k_plane_in(zi, kind):
        block = kb.at[zi, plane[kind][0], c, plane[kind][1]]
        return rc(block, block, ks.at[zi, 2 + kind], kr.at[zi, 1 + kind], peers[kind])

    def k_sib(zi, core, half):
        block = kb.at[zi, halves[half], core]
        return rc(block, block, sks.at[zi, half], skr.at[zi, half], sib)

    sources = (wuk, wuv)
    bufs = (wkb, wvb)

    def w_x(m):
        return rc(
            sources[m].at[:, lanes(1 - x, width)], bufs[m].at[z, x, c], wxs.at[m], wxr.at[m], peers[0]
        )

    halves = (x, 1 - x)

    def w_up(m, half, zi):
        block = bufs[m].at[zi, halves[half], c]
        return rc(block, block, wzs.at[m, half, zi, 0], wr.at[m, half, zi], up)

    def w_down(m, half, zi):
        block = bufs[m].at[zi, halves[half], c]
        return rc(block, block, wzs.at[m, half, zi, 1], wr.at[m, half, zi], down)

    def w_sib(m, zi, core):
        block = bufs[m].at[zi, :, core]
        return rc(block, block, wss.at[m, zi], wsr.at[m, zi], sib)

    def q_send(kind):
        px, pf = plane[kind]
        return rc(
            q.at[:, lanes(pf * 2 + px, q_width)], qb.at[me], qs.at[kind], qr.at[kind], peers[kind]
        )

    def q_in(kind):
        px, pf = plane[kind]
        block = qb.at[px * 2 + pf]
        return rc(block, block, qs.at[kind], qr.at[kind], peers[kind])

    def each_round(step, on_low, on_high):
        pl.when(z - step >= 0)(lambda: on_low(z - step))
        pl.when(z + step < depth)(lambda: on_high(z + step))

    def k_low(zi):
        k_up(zi).wait_recv()
        pl.when(has_up)(lambda: k_up(zi).start())
        for kind in range(3):
            k_plane(zi, kind).start()

    def k_high(zi):
        k_down(zi).wait_recv()
        pl.when(has_down)(lambda: k_down(zi).start())
        for kind in range(3):
            k_plane(zi, kind).start()

    def w_low(m, half, zi):
        w_up(m, half, zi).wait_recv()
        pl.when(has_up)(lambda: w_up(m, half, zi).start())
        if half:
            w_sib(m, zi, c).start()

    def w_high(m, half, zi):
        w_down(m, half, zi).wait_recv()
        pl.when(has_down)(lambda: w_down(m, half, zi).start())
        if half:
            w_sib(m, zi, c).start()

    def k_plane_done(zi):
        k_plane_in(zi, 1).wait_recv()
        k_sib(zi, c, 0).start()
        for kind in (0, 2):
            k_plane_in(zi, kind).wait_recv()
        k_sib(zi, c, 1).start()

    def w_first(m, half):
        if half:
            block = bufs[m].at[z, 1 - x, c]
            rc(block, block, wxs.at[m], wxr.at[m], peers[0]).wait_recv()
            w_sib(m, z, c).start()
        pl.when(has_up)(lambda: w_up(m, half, z).start())
        pl.when(has_down)(lambda: w_down(m, half, z).start())

    order = [(0, 0), (1, 0), (0, 1), (1, 1)]
    w_x(0).start()
    pl.when(has_up)(lambda: k_up(z).start())
    pl.when(has_down)(lambda: k_down(z).start())
    k_plane(z, 1).start()
    w_x(1).start()
    for copy in own:
        copy.wait()
    w_first(0, 0)
    w_first(1, 0)
    q_send(1).start()
    w_first(0, 1)
    k_plane(z, 0).start()
    k_plane(z, 2).start()
    w_first(1, 1)
    q_send(0).start()
    q_send(2).start()
    for step in range(1, depth):
        each_round(step, k_low, k_high)
        for m, half in order:
            each_round(
                step, functools.partial(w_low, m, half), functools.partial(w_high, m, half)
            )
        if step == 1:
            k_plane_done(z)
        else:
            each_round(step - 1, k_plane_done, k_plane_done)
    for kind in range(3):
        q_in(kind).wait_recv()
    for zi in range(depth):
        w_sib(0, zi, 1 - c).wait_recv()

    rows = 4 * SPAN
    tables = []
    places = []
    for px in range(2):
        for pf in range(2):
            held = span[((z * 2 + px) * 2 + c) * 2 + pf]
            tables.append(span_table(coarse[held], fine[...]))
            places.append(held * SPAN + lax.broadcasted_iota(jnp.int32, (SPAN, 1), 0))
    table = [jnp.concatenate(part, axis=0) for part in zip(*tables)]
    query_pos = jnp.concatenate(places, axis=0)
    queries = qb[...].reshape(rows, q_width)
    key_map = wkb[...].reshape(LATENT, width)
    lat, rot = [], []
    for head in range(heads):
        begin = head * (NOPE + ROPE)
        lat.append(
            lax.dot_general(
                queries[:, begin : begin + NOPE],
                key_map[:, head * NOPE : (head + 1) * NOPE],
                (((1,), (1,)), ((), ())),
                preferred_element_type=jnp.float32,
            ).astype(jnp.bfloat16)
        )
        rot.append(turn(queries[:, begin + NOPE : begin + NOPE + ROPE], *table))
    total_keys = depth * 8 * SPAN
    lane = lax.broadcasted_iota(jnp.int32, (1, total_keys), 1)
    key_pos = jnp.zeros((1, total_keys), jnp.int32)
    for slot in range(depth * 8):
        key_pos = jnp.where(lane // SPAN == slot, span[slot] * SPAN, key_pos)
    key_pos = key_pos + lane % SPAN
    allowed = key_pos <= query_pos

    each_round(depth - 1, k_plane_done, k_plane_done)
    for zi in range(depth):
        for half in range(2):
            k_sib(zi, 1 - c, half).wait_recv()

    keys_lat = kb[:, :, :, :, :, :LATENT].reshape(total_keys, LATENT)
    keys_rot = kb[:, :, :, :, :, LATENT:].reshape(total_keys, ROPE)
    scale = 1.0 / math.sqrt(NOPE + ROPE)
    outs = []
    for pair in range(2):
        pick = slice(2 * pair, 2 * pair + 2)
        score = lax.dot_general(
            jnp.concatenate(lat[pick], axis=0), keys_lat,
            (((1,), (1,)), ((), ())), preferred_element_type=jnp.float32,
        ) + lax.dot_general(
            jnp.concatenate(rot[pick], axis=0), keys_rot,
            (((1,), (1,)), ((), ())), preferred_element_type=jnp.float32,
        )
        score = jnp.where(
            allowed[None], score.reshape(2, rows, total_keys) * scale, jnp.float32(-1e30)
        ).reshape(2 * rows, total_keys)
        expo = jnp.exp(score - jnp.max(score, axis=1, keepdims=True))
        totals = jnp.sum(expo, axis=1, keepdims=True)
        accum = jnp.dot(expo.astype(jnp.bfloat16), keys_lat, preferred_element_type=jnp.float32)
        outs.append((accum * (1.0 / totals)).astype(jnp.bfloat16))

    for zi in range(depth):
        w_sib(1, zi, 1 - c).wait_recv()

    value_map = wvb[...].reshape(LATENT, width)
    for head in range(heads):
        part = outs[head // 2][(head % 2) * rows : (head % 2 + 1) * rows]
        ob[:, :, head * VDIM : (head + 1) * VDIM] = (
            jnp.dot(
                part, value_map[:, head * VDIM : (head + 1) * VDIM],
                preferred_element_type=jnp.float32,
            )
            .astype(jnp.bfloat16)
            .reshape(4, SPAN, VDIM)
        )

    def o_send(kind):
        px, pf = plane[kind]
        return rc(
            ob.at[px * 2 + pf], out.at[:, lanes(group, width)], os_.at[kind], or_.at[kind], peers[kind]
        )

    def o_in(kind):
        px, pf = plane[kind]
        block = out.at[:, lanes(pf * 2 + px, width)]
        return rc(block, block, os_.at[kind], or_.at[kind], peers[kind])

    for kind in range(3):
        o_send(kind).start()
    mine = pltpu.make_async_copy(ob.at[me], out.at[:, lanes(group, width)], loc.at[0])
    mine.start()

    for zi in range(depth):
        pl.when(jnp.logical_and(has_up, zi <= z))(lambda zi=zi: k_up(zi).wait_send())
        pl.when(jnp.logical_and(has_down, zi >= z))(lambda zi=zi: k_down(zi).wait_send())
        for kind in range(3):
            k_plane(zi, kind).wait_send()
        for m in range(2):
            for half in range(2):
                pl.when(jnp.logical_and(has_up, zi <= z))(
                    lambda zi=zi, m=m, half=half: w_up(m, half, zi).wait_send()
                )
                pl.when(jnp.logical_and(has_down, zi >= z))(
                    lambda zi=zi, m=m, half=half: w_down(m, half, zi).wait_send()
                )
            w_sib(m, zi, c).wait_send()
    for m in range(2):
        w_x(m).wait_send()
    for zi in range(depth):
        for half in range(2):
            k_sib(zi, c, half).wait_send()
    for kind in range(3):
        q_send(kind).wait_send()
    mine.wait()
    for kind in range(3):
        o_in(kind).wait_recv()
        o_send(kind).wait_send()


def planned(query_heads, kv_latent, w_uk, w_uv, span_order):
    depth = lax.axis_size("ctx") // 4
    local_count = kv_latent.shape[0]
    width = w_uk.shape[1] // 2
    q_width = query_heads.shape[1] // 4
    dma = pltpu.SemaphoreType.DMA
    vmem = pl.BlockSpec(memory_space=pltpu.VMEM)
    spans = span_order.shape[0]
    hbm = pl.BlockSpec(memory_space=pltpu.HBM)
    coarse = jnp.asarray(rope_table(spans, SPAN).reshape(spans, 1, 2 * ROPE))
    fine = jnp.asarray(rope_table(SPAN, 1))
    return pl.pallas_call(
        kernel,
        out_shape=jax.ShapeDtypeStruct((local_count, width * 4), jnp.bfloat16),
        in_specs=[hbm] * 7,
        out_specs=vmem,
        scratch_shapes=[
            pltpu.SMEM((spans,), jnp.int32),
            pltpu.VMEM((spans, 1, 2 * ROPE), jnp.float32),
            pltpu.VMEM((SPAN, 2 * ROPE), jnp.float32),
            pltpu.VMEM((4, SPAN, q_width), jnp.bfloat16),
            pltpu.VMEM((depth, 2, 2, 2, SPAN, LATENT + ROPE), jnp.bfloat16),
            pltpu.VMEM((depth, 2, 2, w_uk.shape[0], width), jnp.bfloat16),
            pltpu.VMEM((depth, 2, 2, w_uk.shape[0], width), jnp.bfloat16),
            pltpu.VMEM((4, SPAN, width), jnp.bfloat16),
            dma((7,)),
            dma((depth, 5)), dma((depth, 4)), dma((depth, 2)), dma((depth, 2)),
            dma((2,)), dma((2,)), dma((2, 2, depth, 2)), dma((2, 2, depth)), dma((2, depth)), dma((2, depth)),
            dma((3,)), dma((3,)), dma((3,)), dma((3,)),
        ],
        compiler_params=pltpu.CompilerParams(
            collective_id=0, has_side_effects=True, vmem_limit_bytes=60 * 1024 * 1024
        ),
        name="mla_prefill",
    )(span_order, query_heads, kv_latent, w_uk, w_uv, coarse, fine)


def solution(mesh):
    placed = (
        P(("ctx", "fsdp"), None),
        P(("ctx", "fsdp"), None),
        P("ctx", "fsdp"),
        P("ctx", "fsdp"),
        P(),
    )
    small = mesh.shape["fsdp"] == 2 and mesh.shape["ctx"] == 16

    def program(query_heads, kv_latent, w_uk, w_uv, span_order):
        fits = (
            small
            and query_heads.shape[1] == 16 * (NOPE + ROPE)
            and query_heads.shape[0] == 32 * SPAN
        )
        return jax.shard_map(
            planned if fits else body,
            mesh=mesh, in_specs=placed, out_specs=P(("ctx", "fsdp"), None), check_vma=False,
        )(query_heads, kv_latent, w_uk, w_uv, span_order)

    return program
```
